32 devices in a mesh: atm: 8 (over z, x), cpl: 4 (over y, core).
Axes of the slice: x: 2, y: 2, z: 4, core: 2. Of those that a mesh axis runs over, the one named last changes fastest.
Arguments:
- state: bfloat16 [16384, 32, 128], P(('atm', 'cpl')), may hold values from -6 to 6
- cosine_zenith: bfloat16 [16384], P(('atm', 'cpl')), may hold values from 0.25 to 1
- sunlit: int32 [16384], P(('atm', 'cpl')), may hold values from 0 to 1, as said below
- kcoef: bfloat16 [32, 256], replicated, may hold values from -1 to 1
- scatter_coef: bfloat16 [32, 256], replicated, may hold values from -1 to 1
- gpoint_weight: float32 [256], replicated, may hold values from 0.3 to 3
- sea_temp: float32 [16384], P(('atm', 'cpl')), may hold values from -6 to 6
- intersection_col: int32 [16384, 4], P(('atm', 'cpl')), may hold values from 0 to 2047
- intersection_weight: int32 [16384, 4], P(('atm', 'cpl')), may hold values from 1 to 8
- nearest_ocean: int32 [16384], P(('atm', 'cpl')), may hold values from 0 to 2047
Outputs:
- heating_rate: float32 [16384, 128], P(('atm', 'cpl'))
- sea_temp_next: float32 [16384], P(('atm', 'cpl'))
- column_sea_temp: float32 [16384], P(('atm', 'cpl'))
The draws below stay inside these ranges and needn't reach their ends.
Inputs may be any that keep to these rules, and one draw needn't show every extreme that they name: On each device the number of sunlit columns is a multiple of 8; the two devices of one cpl index whose atm indices differ by 4 together hold exactly 512 sunlit columns. `intersection_col`: Indexes, in cpl order, the columns held by the 4 devices that share the ocean cell's atm index. `nearest_ocean`: Indexes, in cpl order, the ocean cells held by the 4 devices that share the column's atm index.
All inputs are finite; a program needn't handle non-finite values.
Results may differ from the reference program's by a relative error of at most 0.0006.
Values may be sent and summed in bfloat16 or wider, within the bound.
A program may use at most 64 MiB of HBM per device.

```python
import math
import jax
import jax.numpy as jnp
from jax import lax

LEV = 128
G = 256
FEAT = 32
NOV = 4
COL_DEV = 512
OCN_DEV = 512
COLS = 16384
OCELLS = 16384
N_ATM = 8
N_CPL = 4


def draw_sunlit(key, part):
    per_peer = COL_DEV // N_ATM
    half = N_ATM // 2
    key_rot, key_split, key_cols = jax.random.split(key, 3)
    rotation = jax.random.randint(key_rot, (N_CPL,), 0, N_ATM)
    partial_sun = jax.random.randint(key_split, (N_CPL,), 0, per_peer + 1)
    atm_index = jnp.arange(N_ATM, dtype=jnp.int32)[:, None]
    offset = (atm_index - rotation[None, :]) % N_ATM
    blocks = jnp.where(offset < half - 1, per_peer, 0)
    blocks = jnp.where(offset == half - 1, per_peer - partial_sun[None, :], blocks)
    blocks = jnp.where(offset == N_ATM - 1, partial_sun[None, :], blocks)
    counts = (blocks * N_ATM).reshape(-1)
    device_keys = jax.random.split(key_cols, N_ATM * N_CPL)
    ranks = jax.vmap(lambda single: jax.random.permutation(single, COL_DEV))(device_keys)
    return (ranks < counts[:, None]).astype(jnp.int32).reshape(-1)


def place_ends(entries, own_key, least, high):
    longest = entries.shape.index(max(entries.shape))
    spots = []
    for shift in (0, 1):
        where = [jax.random.randint(jax.random.fold_in(own_key, axis), (), 0, length) for axis, length in enumerate(entries.shape)]
        where[longest] = (where[longest] + shift) % entries.shape[longest]
        spots.append(tuple(where))
    return entries.at[spots[0]].set(least).at[spots[1]].set(high)


def shard_levels(own_key, extent, pieces, low, top_value):
    gain, own = 1.0, jax.random.fold_in(own_key, 6)
    for axis_at, blocks in pieces:
        draws = jnp.exp(jax.random.uniform(jax.random.fold_in(own, axis_at), (blocks,), jnp.float32, low / len(pieces), top_value / len(pieces)))
        gain = gain * jnp.repeat(draws, extent[axis_at] // blocks).reshape([-1 if axis == axis_at else 1 for axis in range(len(extent))])
    return gain


def bell_draw(stream_key, extent, deviation, most, cuts=(), kind=jnp.bfloat16):
    loudness = shard_levels(stream_key, extent, cuts, -0.22, 0.18) if cuts else 1.0
    array = jax.random.normal(stream_key, extent, jnp.float32) * deviation * loudness
    return jnp.minimum(jnp.maximum(array, -most), most).astype(kind)


def setup_inputs(seed: int = 0) -> dict:
    keys = jax.random.split(jax.random.key(seed), 11)
    return {
        "state": bell_draw(keys[0], (COLS, FEAT, LEV), 1.0, 6.0, ((0, 32),)),
        "cosine_zenith": jnp.clip(0.25 + 0.75 * jax.random.uniform(keys[1], (COLS,), jnp.float32) ** shard_levels(keys[1], (COLS,), ((0, 32),), -0.2, 0.2), 0.25, 1.0).astype(jnp.bfloat16),
        "sunlit": draw_sunlit(jax.random.fold_in(keys[10], 71), 0),
        "kcoef": bell_draw(keys[3], (FEAT, G), FEAT ** -0.5, 1.0),
        "scatter_coef": bell_draw(keys[4], (FEAT, G), FEAT ** -0.5, 1.0),
        "gpoint_weight": jnp.clip(jnp.exp(jax.random.uniform(keys[5], (G,), jnp.float32, math.log(0.3), math.log(3.0))), 0.3, 3.0),
        "sea_temp": bell_draw(keys[6], (OCELLS,), 1.0, 6.0, ((0, 32),), jnp.float32),
        "intersection_col": place_ends(jax.random.randint(keys[7], (OCELLS, NOV), 0, N_CPL * COL_DEV), jax.random.fold_in(keys[7], 1), 0, (N_CPL * COL_DEV) - 1).astype(jnp.int32),
        "intersection_weight": place_ends(jax.random.randint(keys[8], (OCELLS, NOV), 1, 9), jax.random.fold_in(keys[8], 1), 1, 8).astype(jnp.int32),
        "nearest_ocean": place_ends(jax.random.randint(keys[9], (COLS,), 0, N_CPL * OCN_DEV), jax.random.fold_in(keys[9], 1), 0, (N_CPL * OCN_DEV) - 1).astype(jnp.int32),
    }


depth_scale = 0.01
relax_keep = 0.75
forcing = 4.0
block_cols = 32


def column_optics(state_blk, cosine_blk, kcoef, scatter_coef, weights):
    levels = state_blk.shape[2]
    gpoints = kcoef.shape[1]
    state32 = state_blk.astype(jnp.float32)
    proj_abs = jnp.einsum("cfl,fg->clg", state32, kcoef.astype(jnp.float32), precision=lax.Precision.HIGHEST)
    proj_sca = jnp.einsum("cfl,fg->clg", state32, scatter_coef.astype(jnp.float32), precision=lax.Precision.HIGHEST)
    soft_abs = jax.nn.softplus(proj_abs)
    soft_sca = jax.nn.softplus(proj_sca)
    extinction = (depth_scale * (soft_abs + soft_sca)).astype(jnp.bfloat16)
    share = soft_abs / (soft_abs + soft_sca)
    row_index = lax.broadcasted_iota(jnp.int32, (levels, levels), 0)
    col_index = lax.broadcasted_iota(jnp.int32, (levels, levels), 1)
    upper = (row_index < col_index).astype(jnp.float32)
    ext32 = extinction.astype(jnp.float32)
    above = jnp.einsum("cmg,ml->clg", ext32, upper, precision=lax.Precision.HIGHEST)
    cosine = cosine_blk.astype(jnp.float32)
    lit_col = cosine > 0.0
    safe_cos = jnp.where(lit_col, cosine, jnp.float32(1.0))
    inverse = 1.0 / safe_cos
    downward = safe_cos[:, None, None] * jnp.exp(-above * inverse[:, None, None])
    absorbed = share * downward * (1.0 - jnp.exp(-ext32 * inverse[:, None, None]))
    heating = jnp.sum(absorbed * weights, axis=-1) * (levels / gpoints)
    bottom = safe_cos[:, None] * jnp.exp(-(above[:, -1, :] + ext32[:, -1, :]) * inverse[:, None])
    surface = jnp.sum(bottom * weights, axis=-1) / gpoints
    heating = jnp.where(lit_col[:, None], heating, jnp.float32(0.0))
    surface = jnp.where(lit_col, surface, jnp.float32(0.0))
    return heating, surface


def reference(state, cosine_zenith, sunlit, kcoef, scatter_coef, gpoint_weight, sea_temp, intersection_col, intersection_weight, nearest_ocean):
    cosine_eff = cosine_zenith * sunlit.astype(cosine_zenith.dtype)
    total = state.shape[0]
    block_count = total // block_cols
    state_blocks = state.reshape(block_count, block_cols, state.shape[1], state.shape[2])
    cosine_blocks = cosine_eff.reshape(block_count, block_cols)

    def one_block(pair):
        return column_optics(pair[0], pair[1], kcoef, scatter_coef, gpoint_weight)

    heating, surface = lax.map(one_block, (state_blocks, cosine_blocks))
    heating = heating.reshape(total, state.shape[2])
    surface = surface.reshape(total)
    cells = sea_temp.shape[0]
    cell_base = (jnp.arange(cells, dtype=jnp.int32) // (OCN_DEV * N_CPL)) * (N_CPL * COL_DEV)
    picked = surface[cell_base[:, None] + intersection_col]
    weight_f = intersection_weight.astype(jnp.float32)
    ocean_flux = jnp.sum(weight_f * picked, axis=-1) / jnp.sum(weight_f, axis=-1)
    sea_next = relax_keep * sea_temp + forcing * ocean_flux
    column_base = (jnp.arange(total, dtype=jnp.int32) // (COL_DEV * N_CPL)) * (N_CPL * OCN_DEV)
    column_sea = sea_next[column_base + nearest_ocean]
    return heating, sea_next, column_sea
```

```python
import functools

import jax
import jax.numpy as jnp
from jax import lax
from jax.experimental import pallas as pl
from jax.experimental.pallas import tpu as pltpu
from jax.sharding import PartitionSpec as P

depth_scale = 0.01
relax_keep = 0.75
forcing = 4.0
log2e = 1.4426950408889634
ln2 = 0.6931471805599453
one_up = 1.0 + 2.0**-23
small_row = 14.0
block_g = 32
first_cols = 16


def radiation_kernel(
    cosine_ref, sunlit_ref, state_hbm, kcoef_ref, scatter_ref, weight_ref,
    heat_ref, surf_ref,
    state_ref, kboth_ref, upper_ref, wide_ref, part_ref,
    proj0, proj1, a0, a1, x0, x1, ext0, ext1, sems,
):
    columns, levels = heat_ref.shape
    gpoints = wide_ref.shape[0]
    pairs = columns // 2
    head = pltpu.make_async_copy(
        state_hbm.at[pl.ds(0, first_cols)], state_ref.at[pl.ds(0, first_cols)], sems.at[0]
    )
    tail = pltpu.make_async_copy(
        state_hbm.at[pl.ds(first_cols, columns - first_cols)],
        state_ref.at[pl.ds(first_cols, columns - first_cols)],
        sems.at[1],
    )
    head.start()
    tail.start()

    for half, ref in enumerate((kcoef_ref, scatter_ref)):
        scaled = ref[...].astype(jnp.float32) * log2e
        high = scaled.astype(jnp.bfloat16).astype(jnp.float32)
        both = jnp.concatenate([high, scaled - high], axis=0)
        kboth_ref[pl.ds(half * gpoints, gpoints), :] = both.T.astype(jnp.bfloat16)
    row_index = lax.broadcasted_iota(jnp.int32, (2 * levels, 2 * levels), 0)
    col_index = lax.broadcasted_iota(jnp.int32, (2 * levels, 2 * levels), 1)
    same = (row_index >= levels) == (col_index >= levels)
    upper = jnp.where(same & (row_index <= col_index), 1.0, 0.0)
    upper_ref[...] = upper.astype(jnp.bfloat16)
    wide_ref[...] = jnp.broadcast_to(weight_ref[...], (2 * levels, gpoints)).T
    reach = jnp.maximum(
        jnp.sum(jnp.abs(kcoef_ref[...].astype(jnp.float32)), axis=0, keepdims=True),
        jnp.sum(jnp.abs(scatter_ref[...].astype(jnp.float32)), axis=0, keepdims=True),
    )
    bounded = jnp.max(reach) <= small_row

    row_id = lax.broadcasted_iota(jnp.int32, (8, 2 * levels), 0)
    lane_id = lax.broadcasted_iota(jnp.int32, (8, 2 * levels), 1)
    left = lane_id < levels
    select = jnp.where((left & (row_id == 0)) | (~left & (row_id == 1)), 1.0, 0.0).astype(jnp.bfloat16)
    row8 = lax.broadcasted_iota(jnp.int32, (8, gpoints), 0)
    start = lax.broadcasted_iota(jnp.int32, (block_g, levels), 1) == 0
    lane1 = lax.broadcasted_iota(jnp.int32, (1, 2 * levels), 1)

    def project(pair, proj):
        base = 2 * jnp.minimum(pair, pairs - 1)
        both = jnp.concatenate([state_ref[base], state_ref[base + 1]], axis=1)
        both = jnp.concatenate([both, both], axis=0)
        proj[...] = jnp.dot(kboth_ref[...], both, preferred_element_type=jnp.float32)

    def soften(clamped, proj, a_ref, x_ref, ext_ref):
        for low in range(0, gpoints, block_g):
            rows = slice(low, low + block_g)
            ta, ts = proj[rows], proj[gpoints + low : gpoints + low + block_g]
            ya = jnp.exp2(jnp.minimum(ta, 24.0) if clamped else ta)
            ys = jnp.exp2(jnp.minimum(ts, 24.0) if clamped else ts)
            soft_abs = jnp.minimum(lax.log2(ya + one_up), ya * log2e)
            soft_sca = lax.log2(ys + one_up)
            if clamped:
                soft_abs = jnp.maximum(ta, soft_abs)
                soft_sca = jnp.maximum(ts, soft_sca)
            soft = soft_abs + soft_sca
            a_ref[rows] = soft_abs * wide_ref[rows]
            x_ref[rows] = soft
            ext_ref[rows] = ((depth_scale * ln2) * soft).astype(jnp.bfloat16)

    def absorb(pair, a_ref, x_ref, ext_ref):
        base = 2 * pair
        lit_first, lit_second = sunlit_ref[base] > 0, sunlit_ref[base + 1] > 0
        u_first = jnp.where(lit_first, cosine_ref[base], 1.0)
        u_second = jnp.where(lit_second, cosine_ref[base + 1], 1.0)
        u_lane = jnp.where(lane1 < levels, u_first, u_second)
        rate = -log2e / u_lane
        out_first = jnp.where(lit_first, u_first, 0.0)
        out_second = jnp.where(lit_second, u_second, 0.0)
        out_lane = jnp.where(lane1 < levels, out_first, out_second)
        through = jnp.dot(ext_ref[...], upper_ref[...], preferred_element_type=jnp.float32)
        total = jnp.zeros((8, 2 * levels), jnp.float32)
        for low in range(0, gpoints, block_g):
            rows = slice(low, low + block_g)
            leave = jnp.exp2(through[rows] * rate)
            enter = jnp.concatenate(
                [
                    jnp.where(start, 1.0, pltpu.roll(leave[:, :levels], 1, 1)),
                    jnp.where(start, 1.0, pltpu.roll(leave[:, levels:], 1, 1)),
                ],
                axis=1,
            )
            top = a_ref[rows] * (enter - leave)
            bottom = x_ref[rows]
            for half in (block_g // 2, block_g // 4):
                top, bottom = (
                    top[:half] * bottom[half:] + top[half:] * bottom[:half],
                    bottom[:half] * bottom[half:],
                )
            total = total + top * pl.reciprocal(bottom, approx=True)
        row = jnp.sum(total, axis=0, keepdims=True) * (out_lane * (levels / gpoints))
        heat_ref[pl.ds(base, 1), :] = row[:, :levels]
        heat_ref[pl.ds(base + 1, 1), :] = row[:, levels:]
        depth = lax.dot_general(
            select, ext_ref[...], (((1,), (1,)), ((), ())), preferred_element_type=jnp.float32
        )
        u_row = jnp.where(row8 == 0, u_first, u_second)
        out_row = jnp.where(row8 == 0, out_first, out_second)
        left_over = out_row * jnp.exp(-depth / u_row) * (weight_ref[...] / gpoints)
        half = left_over[:, : gpoints // 2] + left_over[:, gpoints // 2 :]
        part_ref[pl.ds(base, 1), :] = half[0:1]
        part_ref[pl.ds(base + 1, 1), :] = half[1:2]

    def sweep(clamped):
        project(0, proj0)
        soften(clamped, proj0, a0, x0, ext0)
        project(1, proj1)

        def step(i, carry):
            @pl.when(i == 1)
            def _():
                tail.wait()

            for inner in range(2):
                pair = 4 * i + 2 * inner
                absorb(pair, a0, x0, ext0)
                soften(clamped, proj1, a1, x1, ext1)
                project(pair + 2, proj0)
                absorb(pair + 1, a1, x1, ext1)
                soften(clamped, proj0, a0, x0, ext0)
                project(pair + 3, proj1)
            return carry

        lax.fori_loop(0, pairs // 4, step, jnp.int32(0))

    head.wait()

    @pl.when(bounded)
    def _():
        sweep(False)

    @pl.when(jnp.logical_not(bounded))
    def _():
        sweep(True)

    for block in range(columns // 128):
        piece = part_ref[block * 128 : (block + 1) * 128].T
        surf_ref[block : block + 1, :] = jnp.sum(piece, axis=0, keepdims=True)


vmem = pl.BlockSpec(memory_space=pltpu.VMEM)
smem = pl.BlockSpec(memory_space=pltpu.SMEM)
anywhere = pl.BlockSpec(memory_space=pl.ANY)


def radiation(cosine, sunlit, state, kcoef, scatter_coef, weights):
    columns, feats, levels = state.shape
    gpoints = kcoef.shape[1]
    wide = 2 * levels
    return pl.pallas_call(
        radiation_kernel,
        out_shape=(
            jax.ShapeDtypeStruct((columns, levels), jnp.float32),
            jax.ShapeDtypeStruct((columns // 128, 128), jnp.float32),
        ),
        in_specs=[smem, smem, anywhere, vmem, vmem, vmem],
        out_specs=(vmem, vmem),
        scratch_shapes=[
            pltpu.VMEM((columns, feats, levels), state.dtype),
            pltpu.VMEM((2 * gpoints, 2 * feats), jnp.bfloat16),
            pltpu.VMEM((wide, wide), jnp.bfloat16),
            pltpu.VMEM((gpoints, wide), jnp.float32),
            pltpu.VMEM((columns, gpoints // 2), jnp.float32),
            pltpu.VMEM((2 * gpoints, wide), jnp.float32),
            pltpu.VMEM((2 * gpoints, wide), jnp.float32),
            pltpu.VMEM((gpoints, wide), jnp.float32),
            pltpu.VMEM((gpoints, wide), jnp.float32),
            pltpu.VMEM((gpoints, wide), jnp.float32),
            pltpu.VMEM((gpoints, wide), jnp.float32),
            pltpu.VMEM((gpoints, wide), jnp.bfloat16),
            pltpu.VMEM((gpoints, wide), jnp.bfloat16),
            pltpu.SemaphoreType.DMA((2,)),
        ],
        compiler_params=pltpu.CompilerParams(vmem_limit_bytes=48 * 1024 * 1024),
        cost_estimate=pl.CostEstimate(
            flops=columns * levels * gpoints * 600,
            bytes_accessed=columns * feats * levels * 2,
            transcendentals=columns * levels * gpoints * 6,
        ),
        name="radiation",
    )(cosine, sunlit, state, kcoef, scatter_coef, weights.reshape(1, -1))


def pick(rows, index):
    low = index % 128
    high = index // 128
    found = jnp.zeros(index.shape, jnp.float32)
    for row, line in enumerate(rows):
        line = jnp.broadcast_to(line, index.shape)
        found = jnp.where(high == row, jnp.take_along_axis(line, low, axis=1), found)
    return found


def ocean_kernel(
    flux_ref, icol_ref, iweight_ref, sea_ref, near_ref, next_ref, column_ref,
    flux_all, sea_all, send_flux, recv_flux, send_sea, recv_sea,
):
    sections, rows, _ = flux_all.shape
    me = lax.axis_index("cpl")
    others = [lax.rem(me + step, sections) for step in range(1, sections)]
    barrier = pltpu.get_barrier_semaphore()
    for other in others:
        pl.semaphore_signal(barrier, inc=1, device_id={"cpl": other}, device_id_type=pl.DeviceIdType.MESH)
    pl.semaphore_wait(barrier, sections - 1)

    def spread(block, table, send, recv):
        copies = [
            pltpu.make_async_remote_copy(
                src_ref=block, dst_ref=table.at[me], send_sem=send.at[step], recv_sem=recv.at[step],
                device_id={"cpl": other}, device_id_type=pl.DeviceIdType.MESH,
            )
            for step, other in enumerate(others)
        ]
        for copy in copies:
            copy.start()
        table[me] = block[...]
        return copies

    def lines(table):
        return [table[section, row : row + 1, :] for section in range(sections) for row in range(rows)]

    copies = spread(flux_ref, flux_all, send_flux, recv_flux)
    index = jnp.concatenate([icol_ref[:, 128 * j : 128 * (j + 1)] for j in range(rows)], axis=0)
    weight = jnp.concatenate([iweight_ref[:, 128 * j : 128 * (j + 1)] for j in range(rows)], axis=0)
    weight = weight.astype(jnp.float32)
    overlaps = icol_ref.shape[0]
    for copy in copies:
        copy.wait()
    product = weight * pick(lines(flux_all), index)
    for j in range(rows):
        part = slice(overlaps * j, overlaps * (j + 1))
        top = jnp.sum(product[part], axis=0, keepdims=True)
        bottom = jnp.sum(weight[part], axis=0, keepdims=True)
        next_ref[j : j + 1, :] = relax_keep * sea_ref[j : j + 1, :] + forcing * (top / bottom)
    copies = spread(next_ref, sea_all, send_sea, recv_sea)
    for copy in copies:
        copy.wait()
    column_ref[...] = pick(lines(sea_all), near_ref[...])


def ocean(flux, icol, iweight, sea, near):
    sections = lax.axis_size("cpl")
    shape = jax.ShapeDtypeStruct(sea.shape, jnp.float32)
    table = pltpu.VMEM((sections, *sea.shape), jnp.float32)
    arrivals = pltpu.SemaphoreType.DMA((sections - 1,))
    return pl.pallas_call(
        ocean_kernel,
        out_shape=(shape, jax.ShapeDtypeStruct(near.shape, jnp.float32)),
        in_specs=[vmem] * 5,
        out_specs=(vmem, vmem),
        scratch_shapes=[table, table, arrivals, arrivals, arrivals, arrivals],
        compiler_params=pltpu.CompilerParams(collective_id=0, has_side_effects=True),
        name="ocean",
    )(flux, icol, iweight, sea, near)


def local(
    state, cosine_zenith, sunlit, kcoef, scatter_coef, gpoint_weight, sea_temp,
    intersection_col, intersection_weight, nearest_ocean,
):
    cosine = cosine_zenith.astype(jnp.float32)
    heating, surface = radiation(cosine, sunlit, state, kcoef, scatter_coef, gpoint_weight)
    sea_next, column_sea = ocean(
        surface, intersection_col.T, intersection_weight.T, sea_temp.reshape(-1, 128), nearest_ocean.reshape(-1, 128)
    )
    return (heating, sea_next.reshape(-1), column_sea.reshape(-1))


def solution(mesh):
    both = ("atm", "cpl")
    return jax.shard_map(
        local,
        mesh=mesh,
        in_specs=(
            P(both, None, None), P(both), P(both), P(), P(), P(), P(both),
            P(both, None), P(both, None), P(both),
        ),
        out_specs=(P(both, None), P(both), P(both)),
        check_vma=False,
    )
```

```python
import functools

import jax
import jax.numpy as jnp
from jax import lax
from jax.experimental import pallas as pl
from jax.experimental.pallas import tpu as pltpu
from jax.sharding import PartitionSpec as P

depth_scale = 0.01
relax_keep = 0.75
forcing = 4.0
log2e = 1.4426950408889634
ln2 = 0.6931471805599453
one_up = 1.0 + 2.0**-23
small_row = 14.0
block_g = 32
first_cols = 16


def radiation_kernel(
    cosine_hbm, sunlit_hbm, state_hbm, kcoef_hbm, scatter_hbm, weight_hbm,
    heat_ref, surf_ref,
    cosine_vec, cosine_ref, sunlit_ref, kcoef_ref, scatter_ref, weight_ref, state_ref, kboth_ref, upper_ref, wide_ref, part_ref,
    proj0, proj1, a0, a1, x0, x1, ext0, ext1, cosine_f32, sems,
):
    columns, levels = heat_ref.shape
    gpoints = wide_ref.shape[0]
    pairs = columns // 2
    head = pltpu.make_async_copy(
        state_hbm.at[pl.ds(0, first_cols)], state_ref.at[pl.ds(0, first_cols)], sems.at[0]
    )
    tail = pltpu.make_async_copy(
        state_hbm.at[pl.ds(first_cols, columns - first_cols)],
        state_ref.at[pl.ds(first_cols, columns - first_cols)],
        sems.at[1],
    )
    small = [
        pltpu.make_async_copy(source, target, sems.at[2 + at])
        for at, (source, target) in enumerate(
            (
                (kcoef_hbm, kcoef_ref), (scatter_hbm, scatter_ref), (weight_hbm, weight_ref),
                (cosine_hbm, cosine_vec), (sunlit_hbm, sunlit_ref),
            )
        )
    ]
    for copy in small:
        copy.start()
    head.start()
    tail.start()
    for copy in small:
        copy.wait()
    cosine_wide = cosine_vec[...].astype(jnp.float32)
    cosine_f32[...] = cosine_wide
    scalars = pltpu.make_async_copy(cosine_f32, cosine_ref, sems.at[7])
    scalars.start()

    for half, ref in enumerate((kcoef_ref, scatter_ref)):
        scaled = ref[...].astype(jnp.float32) * log2e
        high = scaled.astype(jnp.bfloat16).astype(jnp.float32)
        both = jnp.concatenate([high, scaled - high], axis=0)
        kboth_ref[pl.ds(half * gpoints, gpoints), :] = both.T.astype(jnp.bfloat16)
    row_index = lax.broadcasted_iota(jnp.int32, (2 * levels, 2 * levels), 0)
    col_index = lax.broadcasted_iota(jnp.int32, (2 * levels, 2 * levels), 1)
    same = (row_index >= levels) == (col_index >= levels)
    upper = jnp.where(same & (row_index <= col_index), 1.0, 0.0)
    upper_ref[...] = upper.astype(jnp.bfloat16)
    wide_ref[...] = jnp.broadcast_to(weight_ref[...], (2 * levels, gpoints)).T
    reach = jnp.maximum(
        jnp.sum(jnp.abs(kcoef_ref[...].astype(jnp.float32)), axis=0, keepdims=True),
        jnp.sum(jnp.abs(scatter_ref[...].astype(jnp.float32)), axis=0, keepdims=True),
    )
    bounded = jnp.max(reach) <= small_row

    row_id = lax.broadcasted_iota(jnp.int32, (8, 2 * levels), 0)
    lane_id = lax.broadcasted_iota(jnp.int32, (8, 2 * levels), 1)
    left = lane_id < levels
    select = jnp.where((left & (row_id == 0)) | (~left & (row_id == 1)), 1.0, 0.0).astype(jnp.bfloat16)
    row8 = lax.broadcasted_iota(jnp.int32, (8, gpoints), 0)
    start = lax.broadcasted_iota(jnp.int32, (block_g, levels), 1) == 0
    lane1 = lax.broadcasted_iota(jnp.int32, (1, 2 * levels), 1)

    def project(pair, proj):
        base = 2 * jnp.minimum(pair, pairs - 1)
        both = jnp.concatenate([state_ref[base], state_ref[base + 1]], axis=1)
        both = jnp.concatenate([both, both], axis=0)
        proj[...] = jnp.dot(kboth_ref[...], both, preferred_element_type=jnp.float32)

    def soften(clamped, proj, a_ref, x_ref, ext_ref):
        for low in range(0, gpoints, block_g):
            rows = slice(low, low + block_g)
            ta, ts = proj[rows], proj[gpoints + low : gpoints + low + block_g]
            ya = jnp.exp2(jnp.minimum(ta, 24.0) if clamped else ta)
            ys = jnp.exp2(jnp.minimum(ts, 24.0) if clamped else ts)
            soft_abs = jnp.minimum(lax.log2(ya + one_up), ya * log2e)
            soft_sca = lax.log2(ys + one_up)
            if clamped:
                soft_abs = jnp.maximum(ta, soft_abs)
                soft_sca = jnp.maximum(ts, soft_sca)
            soft = soft_abs + soft_sca
            a_ref[rows] = soft_abs * wide_ref[rows]
            x_ref[rows] = soft
            ext_ref[rows] = ((depth_scale * ln2) * soft).astype(jnp.bfloat16)

    def absorb(pair, a_ref, x_ref, ext_ref):
        base = 2 * pair
        line, lane = base // 128, lax.rem(base, 128)
        lit_first, lit_second = sunlit_ref[base] > 0, sunlit_ref[base + 1] > 0
        u_first = jnp.where(lit_first, cosine_ref[line, lane], 1.0)
        u_second = jnp.where(lit_second, cosine_ref[line, lane + 1], 1.0)
        u_lane = jnp.where(lane1 < levels, u_first, u_second)
        rate = -log2e / u_lane
        out_first = jnp.where(lit_first, u_first, 0.0)
        out_second = jnp.where(lit_second, u_second, 0.0)
        out_lane = jnp.where(lane1 < levels, out_first, out_second)
        through = jnp.dot(ext_ref[...], upper_ref[...], preferred_element_type=jnp.float32)
        total = jnp.zeros((8, 2 * levels), jnp.float32)
        for low in range(0, gpoints, block_g):
            rows = slice(low, low + block_g)
            leave = jnp.exp2(through[rows] * rate)
            enter = jnp.concatenate(
                [
                    jnp.where(start, 1.0, pltpu.roll(leave[:, :levels], 1, 1)),
                    jnp.where(start, 1.0, pltpu.roll(leave[:, levels:], 1, 1)),
                ],
                axis=1,
            )
            top = a_ref[rows] * (enter - leave)
            bottom = x_ref[rows]
            for half in (block_g // 2, block_g // 4):
                top, bottom = (
                    top[:half] * bottom[half:] + top[half:] * bottom[:half],
                    bottom[:half] * bottom[half:],
                )
            total = total + top * pl.reciprocal(bottom, approx=True)
        row = jnp.sum(total, axis=0, keepdims=True) * (out_lane * (levels / gpoints))
        heat_ref[pl.ds(base, 1), :] = row[:, :levels]
        heat_ref[pl.ds(base + 1, 1), :] = row[:, levels:]
        depth = lax.dot_general(
            select, ext_ref[...], (((1,), (1,)), ((), ())), preferred_element_type=jnp.float32
        )
        u_row = jnp.where(row8 == 0, u_first, u_second)
        out_row = jnp.where(row8 == 0, out_first, out_second)
        left_over = out_row * jnp.exp(-depth / u_row) * (weight_ref[...] / gpoints)
        half = left_over[:, : gpoints // 2] + left_over[:, gpoints // 2 :]
        part_ref[pl.ds(base, 1), :] = half[0:1]
        part_ref[pl.ds(base + 1, 1), :] = half[1:2]

    def sweep(clamped):
        project(0, proj0)
        soften(clamped, proj0, a0, x0, ext0)
        project(1, proj1)

        def step(i, carry):
            @pl.when(i == 1)
            def _():
                tail.wait()

            for inner in range(2):
                pair = 4 * i + 2 * inner
                absorb(pair, a0, x0, ext0)
                soften(clamped, proj1, a1, x1, ext1)
                project(pair + 2, proj0)
                absorb(pair + 1, a1, x1, ext1)
                soften(clamped, proj0, a0, x0, ext0)
                project(pair + 3, proj1)
            return carry

        lax.fori_loop(0, pairs // 4, step, jnp.int32(0))

    scalars.wait()
    head.wait()

    @pl.when(bounded)
    def _():
        sweep(False)

    @pl.when(jnp.logical_not(bounded))
    def _():
        sweep(True)

    for block in range(columns // 128):
        piece = part_ref[block * 128 : (block + 1) * 128].T
        surf_ref[block : block + 1, :] = jnp.sum(piece, axis=0, keepdims=True)


vmem = pl.BlockSpec(memory_space=pltpu.VMEM)
smem = pl.BlockSpec(memory_space=pltpu.SMEM)
anywhere = pl.BlockSpec(memory_space=pl.ANY)


def radiation(cosine, sunlit, state, kcoef, scatter_coef, weights):
    columns, feats, levels = state.shape
    gpoints = kcoef.shape[1]
    wide = 2 * levels
    return pl.pallas_call(
        radiation_kernel,
        out_shape=(
            jax.ShapeDtypeStruct((columns, levels), jnp.float32),
            jax.ShapeDtypeStruct((columns // 128, 128), jnp.float32),
        ),
        in_specs=[anywhere] * 6,
        out_specs=(vmem, vmem),
        scratch_shapes=[
            pltpu.VMEM(cosine.shape, cosine.dtype),
            pltpu.SMEM(cosine.shape, jnp.float32),
            pltpu.SMEM(sunlit.shape, sunlit.dtype),
            pltpu.VMEM(kcoef.shape, kcoef.dtype),
            pltpu.VMEM(kcoef.shape, kcoef.dtype),
            pltpu.VMEM((1, gpoints), jnp.float32),
            pltpu.VMEM((columns, feats, levels), state.dtype),
            pltpu.VMEM((2 * gpoints, 2 * feats), jnp.bfloat16),
            pltpu.VMEM((wide, wide), jnp.bfloat16),
            pltpu.VMEM((gpoints, wide), jnp.float32),
            pltpu.VMEM((columns, gpoints // 2), jnp.float32),
            pltpu.VMEM((2 * gpoints, wide), jnp.float32),
            pltpu.VMEM((2 * gpoints, wide), jnp.float32),
            pltpu.VMEM((gpoints, wide), jnp.float32),
            pltpu.VMEM((gpoints, wide), jnp.float32),
            pltpu.VMEM((gpoints, wide), jnp.float32),
            pltpu.VMEM((gpoints, wide), jnp.float32),
            pltpu.VMEM((gpoints, wide), jnp.bfloat16),
            pltpu.VMEM((gpoints, wide), jnp.bfloat16),
            pltpu.VMEM(cosine.shape, jnp.float32),
            pltpu.SemaphoreType.DMA((8,)),
        ],
        compiler_params=pltpu.CompilerParams(vmem_limit_bytes=60 * 1024 * 1024),
        cost_estimate=pl.CostEstimate(
            flops=columns * levels * gpoints * 600,
            bytes_accessed=columns * feats * levels * 2,
            transcendentals=columns * levels * gpoints * 6,
        ),
        name="radiation",
    )(cosine, sunlit, state, kcoef, scatter_coef, weights.reshape(1, -1))


def pick(rows, index):
    low = index % 128
    high = index // 128
    found = jnp.zeros(index.shape, jnp.float32)
    for row, line in enumerate(rows):
        line = jnp.broadcast_to(line, index.shape)
        found = jnp.where(high == row, jnp.take_along_axis(line, low, axis=1), found)
    return found


def ocean_kernel(
    flux_ref, icol_ref, iweight_ref, sea_ref, near_ref, half_next_ref, half_column_ref,
    next_ref, flux_all, sea_all, send_flux, recv_flux, send_sea, recv_sea,
):
    sections, rows, _ = flux_all.shape
    me = lax.axis_index("cpl")
    others = [lax.rem(me + step, sections) for step in range(1, sections)]
    barrier = pltpu.get_barrier_semaphore()
    for other in others:
        pl.semaphore_signal(barrier, inc=1, device_id={"cpl": other}, device_id_type=pl.DeviceIdType.MESH)
    pl.semaphore_wait(barrier, sections - 1)

    def spread(block, table, send, recv):
        copies = [
            pltpu.make_async_remote_copy(
                src_ref=block, dst_ref=table.at[me], send_sem=send.at[step], recv_sem=recv.at[step],
                device_id={"cpl": other}, device_id_type=pl.DeviceIdType.MESH,
            )
            for step, other in enumerate(others)
        ]
        for copy in copies:
            copy.start()
        table[me] = block[...]
        return copies

    def lines(table):
        return [table[section, row : row + 1, :] for section in range(sections) for row in range(rows)]

    copies = spread(flux_ref, flux_all, send_flux, recv_flux)
    index = jnp.concatenate([icol_ref[:, 128 * j : 128 * (j + 1)] for j in range(rows)], axis=0)
    weight = jnp.concatenate([iweight_ref[:, 128 * j : 128 * (j + 1)] for j in range(rows)], axis=0)
    weight = weight.astype(jnp.float32)
    overlaps = icol_ref.shape[0]
    for copy in copies:
        copy.wait()
    product = weight * pick(lines(flux_all), index)
    for j in range(rows):
        part = slice(overlaps * j, overlaps * (j + 1))
        top = jnp.sum(product[part], axis=0, keepdims=True)
        bottom = jnp.sum(weight[part], axis=0, keepdims=True)
        next_ref[j : j + 1, :] = relax_keep * sea_ref[j : j + 1, :] + forcing * (top / bottom)
    copies = spread(next_ref, sea_all, send_sea, recv_sea)
    for copy in copies:
        copy.wait()
    column = pick(lines(sea_all), near_ref[...])
    half_next_ref[...] = 0.5 * next_ref[...]
    half_column_ref[...] = 0.5 * column


def ocean(flux, icol, iweight, sea, near):
    sections = lax.axis_size("cpl")
    rows, width = sea.shape
    shape = jax.ShapeDtypeStruct(sea.shape, jnp.float32)
    table = pltpu.VMEM((sections, *sea.shape), jnp.float32)
    arrivals = pltpu.SemaphoreType.DMA((sections - 1,))
    return pl.pallas_call(
        ocean_kernel,
        out_shape=(shape, shape),
        in_specs=[vmem] * 5,
        out_specs=(vmem, vmem),
        scratch_shapes=[pltpu.VMEM((rows, width), jnp.float32), table, table, arrivals, arrivals, arrivals, arrivals],
        compiler_params=pltpu.CompilerParams(collective_id=0, has_side_effects=True),
        name="ocean",
    )(flux, icol, iweight, sea, near)


def local(
    state, cosine_zenith, sunlit, kcoef, scatter_coef, gpoint_weight, sea_temp,
    intersection_col, intersection_weight, nearest_ocean,
):
    cosine = cosine_zenith.reshape(-1, 128)
    heating, surface = radiation(cosine, sunlit, state, kcoef, scatter_coef, gpoint_weight)
    half_next, half_column = ocean(
        surface, intersection_col.T, intersection_weight.T, sea_temp.reshape(-1, 128), nearest_ocean.reshape(-1, 128)
    )
    return (heating, 2.0 * half_next.reshape(-1), 2.0 * half_column.reshape(-1))


def solution(mesh):
    both = ("atm", "cpl")
    return jax.shard_map(
        local,
        mesh=mesh,
        in_specs=(
            P(both, None, None), P(both), P(both), P(), P(), P(), P(both),
            P(both, None), P(both, None), P(both),
        ),
        out_specs=(P(both, None), P(both), P(both)),
        check_vma=False,
    )
```

```python
import functools

import jax
import jax.numpy as jnp
from jax import lax
from jax.experimental import pallas as pl
from jax.experimental.pallas import tpu as pltpu
from jax.sharding import PartitionSpec as P

depth_scale = 0.01
relax_keep = 0.75
forcing = 4.0
log2e = 1.4426950408889634
ln2 = 0.6931471805599453
one_up = 1.0 + 2.0**-23
small_row = 14.0
block_g = 32
first_cols = 16


def radiation_kernel(
    cosine_hbm, sunlit_hbm, state_hbm, kcoef_hbm, scatter_hbm, weight_hbm,
    heat_ref, surf_ref,
    cosine_vec, cosine_ref, sunlit_ref, kcoef_ref, scatter_ref, weight_ref, state_ref, kboth_ref, upper_ref, wide_ref, part_ref,
    proj0, proj1, a0, a1, x0, x1, ext0, ext1, cosine_f32, sems,
):
    columns, levels = heat_ref.shape
    gpoints = wide_ref.shape[0]
    pairs = columns // 2
    head = pltpu.make_async_copy(
        state_hbm.at[pl.ds(0, first_cols)], state_ref.at[pl.ds(0, first_cols)], sems.at[0]
    )
    tail = pltpu.make_async_copy(
        state_hbm.at[pl.ds(first_cols, columns - first_cols)],
        state_ref.at[pl.ds(first_cols, columns - first_cols)],
        sems.at[1],
    )
    small = [
        pltpu.make_async_copy(source, target, sems.at[2 + at])
        for at, (source, target) in enumerate(
            (
                (kcoef_hbm, kcoef_ref), (scatter_hbm, scatter_ref), (weight_hbm, weight_ref),
                (cosine_hbm, cosine_vec), (sunlit_hbm, sunlit_ref),
            )
        )
    ]
    for copy in small:
        copy.start()
    head.start()
    tail.start()
    for copy in small:
        copy.wait()
    cosine_wide = cosine_vec[...].astype(jnp.float32)
    cosine_f32[...] = cosine_wide
    scalars = pltpu.make_async_copy(cosine_f32, cosine_ref, sems.at[7])
    scalars.start()

    for half, ref in enumerate((kcoef_ref, scatter_ref)):
        scaled = ref[...].astype(jnp.float32) * log2e
        high = scaled.astype(jnp.bfloat16).astype(jnp.float32)
        both = jnp.concatenate([high, scaled - high], axis=0)
        kboth_ref[pl.ds(half * gpoints, gpoints), :] = both.T.astype(jnp.bfloat16)
    row_index = lax.broadcasted_iota(jnp.int32, (2 * levels, 2 * levels), 0)
    col_index = lax.broadcasted_iota(jnp.int32, (2 * levels, 2 * levels), 1)
    same = (row_index >= levels) == (col_index >= levels)
    upper = jnp.where(same & (row_index <= col_index), 1.0, 0.0)
    upper_ref[...] = upper.astype(jnp.bfloat16)
    wide_ref[...] = jnp.broadcast_to(weight_ref[...], (2 * levels, gpoints)).T
    reach = jnp.maximum(
        jnp.sum(jnp.abs(kcoef_ref[...].astype(jnp.float32)), axis=0, keepdims=True),
        jnp.sum(jnp.abs(scatter_ref[...].astype(jnp.float32)), axis=0, keepdims=True),
    )
    bounded = jnp.max(reach) <= small_row

    row_id = lax.broadcasted_iota(jnp.int32, (8, 2 * levels), 0)
    lane_id = lax.broadcasted_iota(jnp.int32, (8, 2 * levels), 1)
    left = lane_id < levels
    select = jnp.where((left & (row_id == 0)) | (~left & (row_id == 1)), 1.0, 0.0).astype(jnp.bfloat16)
    row8 = lax.broadcasted_iota(jnp.int32, (8, gpoints), 0)
    start = lax.broadcasted_iota(jnp.int32, (block_g, levels), 1) == 0
    lane1 = lax.broadcasted_iota(jnp.int32, (1, 2 * levels), 1)

    def project(pair, proj):
        base = 2 * jnp.minimum(pair, pairs - 1)
        both = jnp.concatenate([state_ref[base], state_ref[base + 1]], axis=1)
        both = jnp.concatenate([both, both], axis=0)
        proj[...] = jnp.dot(kboth_ref[...], both, preferred_element_type=jnp.float32)

    def soften(clamped, proj, a_ref, x_ref, ext_ref):
        for low in range(0, gpoints, block_g):
            rows = slice(low, low + block_g)
            ta, ts = proj[rows], proj[gpoints + low : gpoints + low + block_g]
            ya = jnp.exp2(jnp.minimum(ta, 24.0) if clamped else ta)
            ys = jnp.exp2(jnp.minimum(ts, 24.0) if clamped else ts)
            soft_abs = jnp.minimum(lax.log2(ya + one_up), ya * log2e)
            soft_sca = lax.log2(ys + one_up)
            if clamped:
                soft_abs = jnp.maximum(ta, soft_abs)
                soft_sca = jnp.maximum(ts, soft_sca)
            soft = soft_abs + soft_sca
            a_ref[rows] = soft_abs
            x_ref[rows] = soft
            ext_ref[rows] = ((depth_scale * ln2) * soft).astype(jnp.bfloat16)

    def sun(base):
        line, lane = base // 128, lax.rem(base, 128)
        lit = [sunlit_ref[base + at] > 0 for at in range(2)]
        u = [jnp.where(lit[at], cosine_ref[line, lane + at], 1.0) for at in range(2)]
        return u, [jnp.where(lit[at], u[at], 0.0) for at in range(2)]

    def absorb(pair, a_ref, x_ref, ext_ref):
        base = 2 * pair
        u, out = sun(base)
        rate = -log2e / jnp.where(lane1 < levels, u[0], u[1])
        through = jnp.dot(ext_ref[...], upper_ref[...], preferred_element_type=jnp.float32)
        total = jnp.zeros((8, 2 * levels), jnp.float32)
        for low in range(0, gpoints, block_g):
            rows = slice(low, low + block_g)
            leave = jnp.exp2(through[rows] * rate)
            enter = jnp.concatenate(
                [
                    jnp.where(start, 1.0, pltpu.roll(leave[:, :levels], 1, 1)),
                    jnp.where(start, 1.0, pltpu.roll(leave[:, levels:], 1, 1)),
                ],
                axis=1,
            )
            top = a_ref[rows] * ((enter - leave) * wide_ref[rows])
            bottom = x_ref[rows]
            for half in (block_g // 2, block_g // 4):
                top, bottom = (
                    top[:half] * bottom[half:] + top[half:] * bottom[:half],
                    bottom[:half] * bottom[half:],
                )
            total = total + top * pl.reciprocal(bottom, approx=True)
        out_lane = jnp.where(lane1 < levels, out[0], out[1])
        row = jnp.sum(total, axis=0, keepdims=True) * (out_lane * (levels / gpoints))
        heat_ref[pl.ds(base, 1), :] = row[:, :levels]
        heat_ref[pl.ds(base + 1, 1), :] = row[:, levels:]

    def reach_ground(pair, ext_ref):
        base = 2 * pair
        u, out = sun(base)
        depth = lax.dot_general(
            select, ext_ref[...], (((1,), (1,)), ((), ())), preferred_element_type=jnp.float32
        )
        u_row = jnp.where(row8 == 0, u[0], u[1])
        out_row = jnp.where(row8 == 0, out[0], out[1])
        left_over = out_row * jnp.exp(-depth / u_row) * (weight_ref[...] / gpoints)
        half = left_over[:, : gpoints // 2] + left_over[:, gpoints // 2 :]
        part_ref[pl.ds(base, 1), :] = half[0:1]
        part_ref[pl.ds(base + 1, 1), :] = half[1:2]

    def sweep(clamped):
        project(0, proj0)
        soften(clamped, proj0, a0, x0, ext0)
        project(1, proj1)

        def step(i, carry):
            @pl.when(i == 1)
            def _():
                tail.wait()

            for inner in range(2):
                pair = 4 * i + 2 * inner
                absorb(pair, a0, x0, ext0)
                reach_ground(pair, ext0)
                soften(clamped, proj1, a1, x1, ext1)
                project(pair + 2, proj0)
                absorb(pair + 1, a1, x1, ext1)
                reach_ground(pair + 1, ext1)
                soften(clamped, proj0, a0, x0, ext0)
                project(pair + 3, proj1)
            return carry

        lax.fori_loop(0, pairs // 4, step, jnp.int32(0))

    scalars.wait()
    head.wait()

    @pl.when(bounded)
    def _():
        sweep(False)

    @pl.when(jnp.logical_not(bounded))
    def _():
        sweep(True)

    for block in range(columns // 128):
        piece = part_ref[block * 128 : (block + 1) * 128].T
        surf_ref[block : block + 1, :] = jnp.sum(piece, axis=0, keepdims=True)


vmem = pl.BlockSpec(memory_space=pltpu.VMEM)
smem = pl.BlockSpec(memory_space=pltpu.SMEM)
anywhere = pl.BlockSpec(memory_space=pl.ANY)


def radiation(cosine, sunlit, state, kcoef, scatter_coef, weights):
    columns, feats, levels = state.shape
    gpoints = kcoef.shape[1]
    wide = 2 * levels
    return pl.pallas_call(
        radiation_kernel,
        out_shape=(
            jax.ShapeDtypeStruct((columns, levels), jnp.float32),
            jax.ShapeDtypeStruct((columns // 128, 128), jnp.float32),
        ),
        in_specs=[anywhere] * 6,
        out_specs=(vmem, vmem),
        scratch_shapes=[
            pltpu.VMEM(cosine.shape, cosine.dtype),
            pltpu.SMEM(cosine.shape, jnp.float32),
            pltpu.SMEM(sunlit.shape, sunlit.dtype),
            pltpu.VMEM(kcoef.shape, kcoef.dtype),
            pltpu.VMEM(kcoef.shape, kcoef.dtype),
            pltpu.VMEM((1, gpoints), jnp.float32),
            pltpu.VMEM((columns, feats, levels), state.dtype),
            pltpu.VMEM((2 * gpoints, 2 * feats), jnp.bfloat16),
            pltpu.VMEM((wide, wide), jnp.bfloat16),
            pltpu.VMEM((gpoints, wide), jnp.float32),
            pltpu.VMEM((columns, gpoints // 2), jnp.float32),
            pltpu.VMEM((2 * gpoints, wide), jnp.float32),
            pltpu.VMEM((2 * gpoints, wide), jnp.float32),
            pltpu.VMEM((gpoints, wide), jnp.float32),
            pltpu.VMEM((gpoints, wide), jnp.float32),
            pltpu.VMEM((gpoints, wide), jnp.float32),
            pltpu.VMEM((gpoints, wide), jnp.float32),
            pltpu.VMEM((gpoints, wide), jnp.bfloat16),
            pltpu.VMEM((gpoints, wide), jnp.bfloat16),
            pltpu.VMEM(cosine.shape, jnp.float32),
            pltpu.SemaphoreType.DMA((8,)),
        ],
        compiler_params=pltpu.CompilerParams(vmem_limit_bytes=60 * 1024 * 1024),
        cost_estimate=pl.CostEstimate(
            flops=columns * levels * gpoints * 600,
            bytes_accessed=columns * feats * levels * 2,
            transcendentals=columns * levels * gpoints * 6,
        ),
        name="radiation",
    )(cosine, sunlit, state, kcoef, scatter_coef, weights.reshape(1, -1))


def pick(rows, index):
    low = index % 128
    high = index // 128
    found = jnp.zeros(index.shape, jnp.float32)
    for row, line in enumerate(rows):
        line = jnp.broadcast_to(line, index.shape)
        found = jnp.where(high == row, jnp.take_along_axis(line, low, axis=1), found)
    return found


def ocean_kernel(
    flux_ref, icol_hbm, iweight_hbm, sea_hbm, sea_all,
    flux_all, icol_ref, iweight_ref, sea_ref, next_ref, local_sems, send_flux, recv_flux, send_sea, recv_sea,
):
    sections, rows, _ = flux_all.shape
    me = lax.axis_index("cpl")
    others = [lax.rem(me + step, sections) for step in range(1, sections)]
    barrier = pltpu.get_barrier_semaphore()
    for other in others:
        pl.semaphore_signal(barrier, inc=1, device_id={"cpl": other}, device_id_type=pl.DeviceIdType.MESH)
    fetches = [
        pltpu.make_async_copy(source, target, local_sems.at[at])
        for at, (source, target) in enumerate(
            (
                (icol_hbm, icol_ref), (iweight_hbm, iweight_ref), (sea_hbm, sea_ref), (flux_ref, flux_all.at[me]),
            )
        )
    ]
    for fetch in fetches:
        fetch.start()
    pl.semaphore_wait(barrier, sections - 1)

    def spread(block, table, send, recv):
        copies = [
            pltpu.make_async_remote_copy(
                src_ref=block, dst_ref=table.at[me], send_sem=send.at[step], recv_sem=recv.at[step],
                device_id={"cpl": other}, device_id_type=pl.DeviceIdType.MESH,
            )
            for step, other in enumerate(others)
        ]
        for copy in copies:
            copy.start()
        return copies

    copies = spread(flux_ref, flux_all, send_flux, recv_flux)
    for fetch in fetches:
        fetch.wait()
    index = jnp.concatenate([icol_ref[:, 128 * j : 128 * (j + 1)] for j in range(rows)], axis=0)
    weight = jnp.concatenate([iweight_ref[:, 128 * j : 128 * (j + 1)] for j in range(rows)], axis=0)
    weight = weight.astype(jnp.float32)
    overlaps = icol_ref.shape[0]
    for copy in copies:
        copy.wait()
    lines = [flux_all[section, row : row + 1, :] for section in range(sections) for row in range(rows)]
    product = weight * pick(lines, index)
    for j in range(rows):
        part = slice(overlaps * j, overlaps * (j + 1))
        top = jnp.sum(product[part], axis=0, keepdims=True)
        bottom = jnp.sum(weight[part], axis=0, keepdims=True)
        next_ref[j : j + 1, :] = relax_keep * sea_ref[j : j + 1, :] + forcing * (top / bottom)
    copies = spread(next_ref, sea_all, send_sea, recv_sea)
    sea_all[me] = next_ref[...]
    for copy in copies:
        copy.wait()


def ocean(flux, icol, iweight, sea):
    sections = lax.axis_size("cpl")
    table = (sections, *sea.shape)
    arrivals = pltpu.SemaphoreType.DMA((sections - 1,))
    return pl.pallas_call(
        ocean_kernel,
        out_shape=jax.ShapeDtypeStruct(table, jnp.float32),
        in_specs=[anywhere] * 4,
        out_specs=vmem,
        scratch_shapes=[
            pltpu.VMEM(table, jnp.float32),
            pltpu.VMEM(icol.shape, icol.dtype),
            pltpu.VMEM(iweight.shape, iweight.dtype),
            pltpu.VMEM(sea.shape, jnp.float32),
            pltpu.VMEM(sea.shape, jnp.float32),
            pltpu.SemaphoreType.DMA((4,)),
            arrivals, arrivals, arrivals, arrivals,
        ],
        compiler_params=pltpu.CompilerParams(
            collective_id=0, has_side_effects=True, vmem_limit_bytes=60 * 1024 * 1024
        ),
        name="ocean",
    )(flux, icol, iweight, sea)


def column_kernel(sea_all, near_ref, next_ref, column_ref):
    sections, rows, _ = sea_all.shape
    next_ref[...] = sea_all[lax.axis_index("cpl")]
    lines = [sea_all[section, row : row + 1, :] for section in range(sections) for row in range(rows)]
    column_ref[...] = pick(lines, near_ref[...])


def column(sea_all, near):
    shape = jax.ShapeDtypeStruct(sea_all.shape[1:], jnp.float32)
    return pl.pallas_call(
        column_kernel,
        out_shape=(shape, jax.ShapeDtypeStruct(near.shape, jnp.float32)),
        in_specs=[vmem] * 2,
        out_specs=(vmem, vmem),
        compiler_params=pltpu.CompilerParams(vmem_limit_bytes=60 * 1024 * 1024),
        name="column",
    )(sea_all, near)


def local(
    state, cosine_zenith, sunlit, kcoef, scatter_coef, gpoint_weight, sea_temp,
    intersection_col, intersection_weight, nearest_ocean,
):
    cosine = cosine_zenith.reshape(-1, 128)
    heating, surface = radiation(cosine, sunlit, state, kcoef, scatter_coef, gpoint_weight)
    sea_all = ocean(surface, intersection_col.T, intersection_weight.T, sea_temp.reshape(-1, 128))
    sea_next, column_sea = column(sea_all, nearest_ocean.reshape(-1, 128))
    return (heating, sea_next.reshape(-1), column_sea.reshape(-1))


def solution(mesh):
    both = ("atm", "cpl")
    return jax.shard_map(
        local,
        mesh=mesh,
        in_specs=(
            P(both, None, None), P(both), P(both), P(), P(), P(), P(both),
            P(both, None), P(both, None), P(both),
        ),
        out_specs=(P(both, None), P(both), P(both)),
        check_vma=False,
    )
```

```python
import functools

import jax
import jax.numpy as jnp
from jax import lax
from jax.experimental import pallas as pl
from jax.experimental.pallas import tpu as pltpu
from jax.sharding import PartitionSpec as P

depth_scale = 0.01
relax_keep = 0.75
forcing = 4.0
log2e = 1.4426950408889634
ln2 = 0.6931471805599453
one_up = 1.0 + 2.0**-23
small_row = 14.0
block_g = 32
unroll = 8
first_cols = 64


def radiation_kernel(
    cosine_hbm, sunlit_hbm, state_hbm, kcoef_hbm, scatter_hbm, weight_hbm,
    heat_ref, surf_ref,
    cosine_vec, cosine_ref, sunlit_ref, kcoef_ref, scatter_ref, weight_ref, state_ref, kboth_ref, upper_ref, wide_ref, part_ref,
    proj0, proj1, a0, a1, x0, x1, ext0, ext1, rate_ref, cosine_f32, sems,
):
    columns, levels = heat_ref.shape
    gpoints = wide_ref.shape[0]
    pairs = columns // 2
    head = pltpu.make_async_copy(
        state_hbm.at[pl.ds(0, first_cols)], state_ref.at[pl.ds(0, first_cols)], sems.at[0]
    )
    tail = pltpu.make_async_copy(
        state_hbm.at[pl.ds(first_cols, columns - first_cols)],
        state_ref.at[pl.ds(first_cols, columns - first_cols)],
        sems.at[1],
    )
    small = [
        pltpu.make_async_copy(source, target, sems.at[2 + at])
        for at, (source, target) in enumerate(
            (
                (kcoef_hbm, kcoef_ref), (scatter_hbm, scatter_ref), (weight_hbm, weight_ref),
                (cosine_hbm, cosine_vec), (sunlit_hbm, sunlit_ref),
            )
        )
    ]
    for copy in small:
        copy.start()
    head.start()
    tail.start()
    for copy in small:
        copy.wait()
    cosine_wide = cosine_vec[...].astype(jnp.float32)
    cosine_f32[...] = cosine_wide
    scalars = pltpu.make_async_copy(cosine_f32, cosine_ref, sems.at[7])
    scalars.start()

    for half, ref in enumerate((kcoef_ref, scatter_ref)):
        scaled = ref[...].astype(jnp.float32) * log2e
        high = scaled.astype(jnp.bfloat16).astype(jnp.float32)
        both = jnp.concatenate([high, scaled - high], axis=0)
        kboth_ref[pl.ds(half * gpoints, gpoints), :] = both.T.astype(jnp.bfloat16)
    row_index = lax.broadcasted_iota(jnp.int32, (2 * levels, 2 * levels), 0)
    col_index = lax.broadcasted_iota(jnp.int32, (2 * levels, 2 * levels), 1)
    same = (row_index >= levels) == (col_index >= levels)
    upper = jnp.where(same & (row_index <= col_index), 1.0, 0.0)
    upper_ref[...] = upper.astype(jnp.bfloat16)
    wide_ref[...] = jnp.broadcast_to(weight_ref[...], (2 * levels, gpoints)).T
    reach = jnp.maximum(
        jnp.sum(jnp.abs(kcoef_ref[...].astype(jnp.float32)), axis=0, keepdims=True),
        jnp.sum(jnp.abs(scatter_ref[...].astype(jnp.float32)), axis=0, keepdims=True),
    )
    bounded = jnp.max(reach) <= small_row

    row_id = lax.broadcasted_iota(jnp.int32, (8, 2 * levels), 0)
    lane_id = lax.broadcasted_iota(jnp.int32, (8, 2 * levels), 1)
    left = lane_id < levels
    select = jnp.where((left & (row_id == 0)) | (~left & (row_id == 1)), 1.0, 0.0).astype(jnp.bfloat16)
    row8 = lax.broadcasted_iota(jnp.int32, (8, gpoints), 0)
    start = lax.broadcasted_iota(jnp.int32, (block_g, levels), 1) == 0
    lane1 = lax.broadcasted_iota(jnp.int32, (1, 2 * levels), 1)
    lane8 = lax.broadcasted_iota(jnp.int32, (8, 2 * levels), 1)

    def project(pair, proj):
        base = 2 * jnp.minimum(pair, pairs - 1)
        both = jnp.concatenate([state_ref[base], state_ref[base + 1]], axis=1)
        both = jnp.concatenate([both, both], axis=0)
        proj[...] = jnp.dot(kboth_ref[...], both, preferred_element_type=jnp.float32)

    def soften(clamped, proj, a_ref, x_ref, ext_ref):
        for low in range(0, gpoints, block_g):
            rows = slice(low, low + block_g)
            ta, ts = proj[rows], proj[gpoints + low : gpoints + low + block_g]
            ya = jnp.exp2(jnp.minimum(ta, 24.0) if clamped else ta)
            ys = jnp.exp2(jnp.minimum(ts, 24.0) if clamped else ts)
            soft_abs = jnp.minimum(lax.log2(ya + one_up), ya * log2e)
            soft_sca = lax.log2(ys + one_up)
            if clamped:
                soft_abs = jnp.maximum(ta, soft_abs)
                soft_sca = jnp.maximum(ts, soft_sca)
            soft = soft_abs + soft_sca
            a_ref[rows] = soft_abs
            x_ref[rows] = soft
            ext_ref[rows] = ((depth_scale * ln2) * soft).astype(jnp.bfloat16)

    def sun(base):
        line, lane = base // 128, lax.rem(base, 128)
        lit = [sunlit_ref[base + at] > 0 for at in range(2)]
        u = [jnp.where(lit[at], cosine_ref[line, lane + at], 1.0) for at in range(2)]
        return u, [jnp.where(lit[at], u[at], 0.0) for at in range(2)]

    def rates(first, count, bank):
        for at in range(count):
            u, _ = sun(2 * jnp.minimum(first + at, pairs - 1))
            rate_ref[bank, at] = -log2e / jnp.where(lane8 < levels, u[0], u[1])

    def absorb(pair, bank, at, a_ref, x_ref, ext_ref):
        base = 2 * pair
        _, out = sun(base)
        through = jnp.dot(ext_ref[...], upper_ref[...], preferred_element_type=jnp.float32)
        total = jnp.zeros((8, 2 * levels), jnp.float32)
        for low in range(0, gpoints, block_g):
            rows = slice(low, low + block_g)
            depth = through[rows].reshape(block_g // 8, 8, 2 * levels)
            leave = jnp.exp2((depth * rate_ref[bank, at][None]).reshape(block_g, 2 * levels))
            enter = jnp.concatenate(
                [
                    jnp.where(start, 1.0, pltpu.roll(leave[:, :levels], 1, 1)),
                    jnp.where(start, 1.0, pltpu.roll(leave[:, levels:], 1, 1)),
                ],
                axis=1,
            )
            top = a_ref[rows] * ((enter - leave) * wide_ref[rows])
            bottom = x_ref[rows]
            for half in (block_g // 2, block_g // 4):
                top, bottom = (
                    top[:half] * bottom[half:] + top[half:] * bottom[:half],
                    bottom[:half] * bottom[half:],
                )
            total = total + top * pl.reciprocal(bottom, approx=True)
        out_lane = jnp.where(lane1 < levels, out[0], out[1])
        row = jnp.sum(total, axis=0, keepdims=True) * (out_lane * (levels / gpoints))
        heat_ref[pl.ds(base, 1), :] = row[:, :levels]
        heat_ref[pl.ds(base + 1, 1), :] = row[:, levels:]

    def reach_ground(pair, ext_ref):
        base = 2 * pair
        u, out = sun(base)
        depth = lax.dot_general(
            select, ext_ref[...], (((1,), (1,)), ((), ())), preferred_element_type=jnp.float32
        )
        u_row = jnp.where(row8 == 0, u[0], u[1])
        out_row = jnp.where(row8 == 0, out[0], out[1])
        left_over = out_row * jnp.exp(-depth / u_row) * (weight_ref[...] / gpoints)
        half = left_over[:, : gpoints // 2] + left_over[:, gpoints // 2 :]
        part_ref[pl.ds(base, 1), :] = half[0:1]
        part_ref[pl.ds(base + 1, 1), :] = half[1:2]

    def sweep(clamped, together):
        projs, sets = (proj0, proj1), ((a0, x0, ext0), (a1, x1, ext1))
        rates(0, together, 0)
        project(0, projs[0])
        soften(clamped, projs[0], *sets[0])
        project(1, projs[1])

        def step(i, carry):
            @pl.when(i == 1)
            def _():
                tail.wait()

            bank = lax.rem(i, 2)
            for at in range(together):
                pair, now, later = together * i + at, at % 2, (at + 1) % 2
                absorb(pair, bank, at, *sets[now])
                reach_ground(pair, sets[now][2])
                soften(clamped, projs[later], *sets[later])
                project(pair + 2, projs[now])
                if at == 0:
                    rates(together * (i + 1), together, 1 - bank)
            return carry

        lax.fori_loop(0, pairs // together, step, jnp.int32(0))

    scalars.wait()
    head.wait()

    @pl.when(bounded)
    def _():
        sweep(False, unroll)

    @pl.when(jnp.logical_not(bounded))
    def _():
        sweep(True, 2)

    for block in range(columns // 128):
        piece = part_ref[block * 128 : (block + 1) * 128].T
        surf_ref[block : block + 1, :] = jnp.sum(piece, axis=0, keepdims=True)


vmem = pl.BlockSpec(memory_space=pltpu.VMEM)
smem = pl.BlockSpec(memory_space=pltpu.SMEM)
anywhere = pl.BlockSpec(memory_space=pl.ANY)


def radiation(cosine, sunlit, state, kcoef, scatter_coef, weights):
    columns, feats, levels = state.shape
    gpoints = kcoef.shape[1]
    wide = 2 * levels
    return pl.pallas_call(
        radiation_kernel,
        out_shape=(
            jax.ShapeDtypeStruct((columns, levels), jnp.float32),
            jax.ShapeDtypeStruct((columns // 128, 128), jnp.float32),
        ),
        in_specs=[anywhere] * 6,
        out_specs=(vmem, vmem),
        scratch_shapes=[
            pltpu.VMEM(cosine.shape, cosine.dtype),
            pltpu.SMEM(cosine.shape, jnp.float32),
            pltpu.SMEM(sunlit.shape, sunlit.dtype),
            pltpu.VMEM(kcoef.shape, kcoef.dtype),
            pltpu.VMEM(kcoef.shape, kcoef.dtype),
            pltpu.VMEM((1, gpoints), jnp.float32),
            pltpu.VMEM((columns, feats, levels), state.dtype),
            pltpu.VMEM((2 * gpoints, 2 * feats), jnp.bfloat16),
            pltpu.VMEM((wide, wide), jnp.bfloat16),
            pltpu.VMEM((gpoints, wide), jnp.float32),
            pltpu.VMEM((columns, gpoints // 2), jnp.float32),
            pltpu.VMEM((2 * gpoints, wide), jnp.float32),
            pltpu.VMEM((2 * gpoints, wide), jnp.float32),
            pltpu.VMEM((gpoints, wide), jnp.float32),
            pltpu.VMEM((gpoints, wide), jnp.float32),
            pltpu.VMEM((gpoints, wide), jnp.float32),
            pltpu.VMEM((gpoints, wide), jnp.float32),
            pltpu.VMEM((gpoints, wide), jnp.bfloat16),
            pltpu.VMEM((gpoints, wide), jnp.bfloat16),
            pltpu.VMEM((2, unroll, 8, wide), jnp.float32),
            pltpu.VMEM(cosine.shape, jnp.float32),
            pltpu.SemaphoreType.DMA((8,)),
        ],
        compiler_params=pltpu.CompilerParams(vmem_limit_bytes=60 * 1024 * 1024),
        cost_estimate=pl.CostEstimate(
            flops=columns * levels * gpoints * 600,
            bytes_accessed=columns * feats * levels * 2,
            transcendentals=columns * levels * gpoints * 6,
        ),
        name="radiation",
    )(cosine, sunlit, state, kcoef, scatter_coef, weights.reshape(1, -1))


def pick(rows, index):
    low = index % 128
    high = index // 128
    found = jnp.zeros(index.shape, jnp.float32)
    for row, line in enumerate(rows):
        line = jnp.broadcast_to(line, index.shape)
        found = jnp.where(high == row, jnp.take_along_axis(line, low, axis=1), found)
    return found


def ocean_kernel(
    flux_ref, icol_hbm, iweight_hbm, sea_hbm, sea_all,
    flux_all, icol_ref, iweight_ref, sea_ref, next_ref, local_sems, send_flux, recv_flux, send_sea, recv_sea,
):
    sections, rows, _ = flux_all.shape
    me = lax.axis_index("cpl")
    others = [lax.rem(me + step, sections) for step in range(1, sections)]
    barrier = pltpu.get_barrier_semaphore()
    for other in others:
        pl.semaphore_signal(barrier, inc=1, device_id={"cpl": other}, device_id_type=pl.DeviceIdType.MESH)
    fetches = [
        pltpu.make_async_copy(source, target, local_sems.at[at])
        for at, (source, target) in enumerate(
            (
                (icol_hbm, icol_ref), (iweight_hbm, iweight_ref), (sea_hbm, sea_ref), (flux_ref, flux_all.at[me]),
            )
        )
    ]
    for fetch in fetches:
        fetch.start()
    pl.semaphore_wait(barrier, sections - 1)

    def spread(block, table, send, recv):
        copies = [
            pltpu.make_async_remote_copy(
                src_ref=block, dst_ref=table.at[me], send_sem=send.at[step], recv_sem=recv.at[step],
                device_id={"cpl": other}, device_id_type=pl.DeviceIdType.MESH,
            )
            for step, other in enumerate(others)
        ]
        for copy in copies:
            copy.start()
        return copies

    copies = spread(flux_ref, flux_all, send_flux, recv_flux)
    for fetch in fetches:
        fetch.wait()
    index = jnp.concatenate([icol_ref[:, 128 * j : 128 * (j + 1)] for j in range(rows)], axis=0)
    weight = jnp.concatenate([iweight_ref[:, 128 * j : 128 * (j + 1)] for j in range(rows)], axis=0)
    weight = weight.astype(jnp.float32)
    overlaps = icol_ref.shape[0]
    for copy in copies:
        copy.wait()
    lines = [flux_all[section, row : row + 1, :] for section in range(sections) for row in range(rows)]
    product = weight * pick(lines, index)
    for j in range(rows):
        part = slice(overlaps * j, overlaps * (j + 1))
        top = jnp.sum(product[part], axis=0, keepdims=True)
        bottom = jnp.sum(weight[part], axis=0, keepdims=True)
        next_ref[j : j + 1, :] = relax_keep * sea_ref[j : j + 1, :] + forcing * (top / bottom)
    copies = spread(next_ref, sea_all, send_sea, recv_sea)
    sea_all[me] = next_ref[...]
    for copy in copies:
        copy.wait()


def ocean(flux, icol, iweight, sea):
    sections = lax.axis_size("cpl")
    table = (sections, *sea.shape)
    arrivals = pltpu.SemaphoreType.DMA((sections - 1,))
    return pl.pallas_call(
        ocean_kernel,
        out_shape=jax.ShapeDtypeStruct(table, jnp.float32),
        in_specs=[anywhere] * 4,
        out_specs=vmem,
        scratch_shapes=[
            pltpu.VMEM(table, jnp.float32),
            pltpu.VMEM(icol.shape, icol.dtype),
            pltpu.VMEM(iweight.shape, iweight.dtype),
            pltpu.VMEM(sea.shape, jnp.float32),
            pltpu.VMEM(sea.shape, jnp.float32),
            pltpu.SemaphoreType.DMA((4,)),
            arrivals, arrivals, arrivals, arrivals,
        ],
        compiler_params=pltpu.CompilerParams(
            collective_id=0, has_side_effects=True, vmem_limit_bytes=60 * 1024 * 1024
        ),
        name="ocean",
    )(flux, icol, iweight, sea)


def column_kernel(sea_all, near_ref, next_ref, column_ref):
    sections, rows, _ = sea_all.shape
    next_ref[...] = sea_all[lax.axis_index("cpl")]
    lines = [sea_all[section, row : row + 1, :] for section in range(sections) for row in range(rows)]
    column_ref[...] = pick(lines, near_ref[...])


def column(sea_all, near):
    shape = jax.ShapeDtypeStruct(sea_all.shape[1:], jnp.float32)
    return pl.pallas_call(
        column_kernel,
        out_shape=(shape, jax.ShapeDtypeStruct(near.shape, jnp.float32)),
        in_specs=[vmem] * 2,
        out_specs=(vmem, vmem),
        compiler_params=pltpu.CompilerParams(vmem_limit_bytes=60 * 1024 * 1024),
        name="column",
    )(sea_all, near)


def local(
    state, cosine_zenith, sunlit, kcoef, scatter_coef, gpoint_weight, sea_temp,
    intersection_col, intersection_weight, nearest_ocean,
):
    cosine = cosine_zenith.reshape(-1, 128)
    heating, surface = radiation(cosine, sunlit, state, kcoef, scatter_coef, gpoint_weight)
    sea_all = ocean(surface, intersection_col.T, intersection_weight.T, sea_temp.reshape(-1, 128))
    sea_next, column_sea = column(sea_all, nearest_ocean.reshape(-1, 128))
    return (heating, sea_next.reshape(-1), column_sea.reshape(-1))


def solution(mesh):
    both = ("atm", "cpl")
    return jax.shard_map(
        local,
        mesh=mesh,
        in_specs=(
            P(both, None, None), P(both), P(both), P(), P(), P(), P(both),
            P(both, None), P(both, None), P(both),
        ),
        out_specs=(P(both, None), P(both), P(both)),
        check_vma=False,
    )
```

```python
import functools

import jax
import jax.numpy as jnp
from jax import lax
from jax.experimental import pallas as pl
from jax.experimental.pallas import tpu as pltpu
from jax.sharding import PartitionSpec as P

depth_scale = 0.01
relax_keep = 0.75
forcing = 4.0
log2e = 1.4426950408889634
ln2 = 0.6931471805599453
one_up = 1.0 + 2.0**-23
small_row = 14.0
block_g = 32
unroll = 8
first_cols = 64


def radiation_kernel(
    cosine_hbm, sunlit_hbm, state_hbm, kcoef_hbm, scatter_hbm, weight_hbm,
    heat_ref, surf_ref,
    cosine_vec, cosine_ref, sunlit_ref, kcoef_ref, scatter_ref, weight_ref, state_ref, kboth_ref, upper_ref, wide_ref, part_ref,
    proj0, proj1, a0, a1, x0, x1, ext0, ext1, rate_ref, cosine_f32, sems,
):
    columns, levels = heat_ref.shape
    gpoints = wide_ref.shape[0]
    pairs = columns // 2
    head = pltpu.make_async_copy(
        state_hbm.at[pl.ds(0, first_cols)], state_ref.at[pl.ds(0, first_cols)], sems.at[0]
    )
    tail = pltpu.make_async_copy(
        state_hbm.at[pl.ds(first_cols, columns - first_cols)],
        state_ref.at[pl.ds(first_cols, columns - first_cols)],
        sems.at[1],
    )
    small = [
        pltpu.make_async_copy(source, target, sems.at[2 + at])
        for at, (source, target) in enumerate(
            (
                (kcoef_hbm, kcoef_ref), (scatter_hbm, scatter_ref), (weight_hbm, weight_ref),
                (cosine_hbm, cosine_vec), (sunlit_hbm, sunlit_ref),
            )
        )
    ]
    for copy in small:
        copy.start()
    head.start()
    tail.start()
    row_index = lax.broadcasted_iota(jnp.int32, (2 * levels, 2 * levels), 0)
    col_index = lax.broadcasted_iota(jnp.int32, (2 * levels, 2 * levels), 1)
    same = (row_index >= levels) == (col_index >= levels)
    upper = jnp.where(same & (row_index <= col_index), 1.0, 0.0)
    upper_ref[...] = upper.astype(jnp.bfloat16)
    for copy in small:
        copy.wait()
    cosine_wide = cosine_vec[...].astype(jnp.float32)
    cosine_f32[...] = cosine_wide
    scalars = pltpu.make_async_copy(cosine_f32, cosine_ref, sems.at[7])
    scalars.start()

    for half, ref in enumerate((kcoef_ref, scatter_ref)):
        scaled = ref[...].astype(jnp.float32) * log2e
        high = scaled.astype(jnp.bfloat16).astype(jnp.float32)
        both = jnp.concatenate([high, scaled - high], axis=0)
        kboth_ref[pl.ds(half * gpoints, gpoints), :] = both.T.astype(jnp.bfloat16)
    wide_ref[...] = jnp.broadcast_to(weight_ref[...], (2 * levels, gpoints)).T
    reach = jnp.maximum(
        jnp.sum(jnp.abs(kcoef_ref[...].astype(jnp.float32)), axis=0, keepdims=True),
        jnp.sum(jnp.abs(scatter_ref[...].astype(jnp.float32)), axis=0, keepdims=True),
    )
    bounded = jnp.max(reach) <= small_row

    row_id = lax.broadcasted_iota(jnp.int32, (8, 2 * levels), 0)
    lane_id = lax.broadcasted_iota(jnp.int32, (8, 2 * levels), 1)
    left = lane_id < levels
    select = jnp.where((left & (row_id == 0)) | (~left & (row_id == 1)), 1.0, 0.0).astype(jnp.bfloat16)
    row8 = lax.broadcasted_iota(jnp.int32, (8, gpoints), 0)
    start = lax.broadcasted_iota(jnp.int32, (block_g, levels), 1) == 0
    lane1 = lax.broadcasted_iota(jnp.int32, (1, 2 * levels), 1)
    lane8 = lax.broadcasted_iota(jnp.int32, (8, 2 * levels), 1)

    def project(pair, proj):
        base = 2 * jnp.minimum(pair, pairs - 1)
        both = jnp.concatenate([state_ref[base], state_ref[base + 1]], axis=1)
        both = jnp.concatenate([both, both], axis=0)
        proj[...] = jnp.dot(kboth_ref[...], both, preferred_element_type=jnp.float32)

    def soften(clamped, proj, a_ref, x_ref, ext_ref):
        for low in range(0, gpoints, block_g):
            rows = slice(low, low + block_g)
            ta, ts = proj[rows], proj[gpoints + low : gpoints + low + block_g]
            ya = jnp.exp2(jnp.minimum(ta, 24.0) if clamped else ta)
            ys = jnp.exp2(jnp.minimum(ts, 24.0) if clamped else ts)
            soft_abs = jnp.minimum(lax.log2(ya + one_up), ya * log2e)
            soft_sca = lax.log2(ys + one_up)
            if clamped:
                soft_abs = jnp.maximum(ta, soft_abs)
                soft_sca = jnp.maximum(ts, soft_sca)
            soft = soft_abs + soft_sca
            a_ref[rows] = soft_abs
            x_ref[rows] = soft
            ext_ref[rows] = ((depth_scale * ln2) * soft).astype(jnp.bfloat16)

    def sun(base):
        line, lane = base // 128, lax.rem(base, 128)
        lit = [sunlit_ref[base + at] > 0 for at in range(2)]
        u = [jnp.where(lit[at], cosine_ref[line, lane + at], 1.0) for at in range(2)]
        return u, [jnp.where(lit[at], u[at], 0.0) for at in range(2)]

    def rates(first, count, bank):
        for at in range(count):
            u, _ = sun(2 * jnp.minimum(first + at, pairs - 1))
            rate_ref[bank, at] = -log2e / jnp.where(lane8 < levels, u[0], u[1])

    def absorb(pair, bank, at, a_ref, x_ref, ext_ref):
        base = 2 * pair
        _, out = sun(base)
        through = jnp.dot(ext_ref[...], upper_ref[...], preferred_element_type=jnp.float32)
        total = jnp.zeros((8, 2 * levels), jnp.float32)
        for low in range(0, gpoints, block_g):
            rows = slice(low, low + block_g)
            depth = through[rows].reshape(block_g // 8, 8, 2 * levels)
            leave = jnp.exp2((depth * rate_ref[bank, at][None]).reshape(block_g, 2 * levels))
            enter = jnp.concatenate(
                [
                    jnp.where(start, 1.0, pltpu.roll(leave[:, :levels], 1, 1)),
                    jnp.where(start, 1.0, pltpu.roll(leave[:, levels:], 1, 1)),
                ],
                axis=1,
            )
            top = a_ref[rows] * ((enter - leave) * wide_ref[rows])
            bottom = x_ref[rows]
            for half in (block_g // 2, block_g // 4):
                top, bottom = (
                    top[:half] * bottom[half:] + top[half:] * bottom[:half],
                    bottom[:half] * bottom[half:],
                )
            total = total + top * pl.reciprocal(bottom, approx=True)
        out_lane = jnp.where(lane1 < levels, out[0], out[1])
        row = jnp.sum(total, axis=0, keepdims=True) * (out_lane * (levels / gpoints))
        heat_ref[pl.ds(base, 1), :] = row[:, :levels]
        heat_ref[pl.ds(base + 1, 1), :] = row[:, levels:]

    def reach_ground(pair, ext_ref):
        base = 2 * pair
        u, out = sun(base)
        depth = lax.dot_general(
            select, ext_ref[...], (((1,), (1,)), ((), ())), preferred_element_type=jnp.float32
        )
        u_row = jnp.where(row8 == 0, u[0], u[1])
        out_row = jnp.where(row8 == 0, out[0], out[1])
        left_over = out_row * jnp.exp(-depth / u_row) * (weight_ref[...] / gpoints)
        half = left_over[:, : gpoints // 2] + left_over[:, gpoints // 2 :]
        part_ref[pl.ds(base, 1), :] = half[0:1]
        part_ref[pl.ds(base + 1, 1), :] = half[1:2]

    def sweep(clamped, together):
        projs, sets = (proj0, proj1), ((a0, x0, ext0), (a1, x1, ext1))
        rates(0, together, 0)
        project(0, projs[0])
        soften(clamped, projs[0], *sets[0])
        project(1, projs[1])

        def step(i, carry):
            @pl.when(i == 1)
            def _():
                tail.wait()

            bank = lax.rem(i, 2)
            for at in range(together):
                pair, now, later = together * i + at, at % 2, (at + 1) % 2
                absorb(pair, bank, at, *sets[now])
                reach_ground(pair, sets[now][2])
                soften(clamped, projs[later], *sets[later])
                project(pair + 2, projs[now])
                if at == 0:
                    rates(together * (i + 1), together, 1 - bank)
            return carry

        lax.fori_loop(0, pairs // together, step, jnp.int32(0))

    scalars.wait()
    head.wait()

    @pl.when(bounded)
    def _():
        sweep(False, unroll)

    @pl.when(jnp.logical_not(bounded))
    def _():
        sweep(True, 2)

    for block in range(columns // 128):
        piece = part_ref[block * 128 : (block + 1) * 128].T
        surf_ref[block : block + 1, :] = jnp.sum(piece, axis=0, keepdims=True)


vmem = pl.BlockSpec(memory_space=pltpu.VMEM)
smem = pl.BlockSpec(memory_space=pltpu.SMEM)
anywhere = pl.BlockSpec(memory_space=pl.ANY)


def radiation(cosine, sunlit, state, kcoef, scatter_coef, weights):
    columns, feats, levels = state.shape
    gpoints = kcoef.shape[1]
    wide = 2 * levels
    return pl.pallas_call(
        radiation_kernel,
        out_shape=(
            jax.ShapeDtypeStruct((columns, levels), jnp.float32),
            jax.ShapeDtypeStruct((columns // 128, 128), jnp.float32),
        ),
        in_specs=[anywhere] * 6,
        out_specs=(vmem, vmem),
        scratch_shapes=[
            pltpu.VMEM(cosine.shape, cosine.dtype),
            pltpu.SMEM(cosine.shape, jnp.float32),
            pltpu.SMEM(sunlit.shape, sunlit.dtype),
            pltpu.VMEM(kcoef.shape, kcoef.dtype),
            pltpu.VMEM(kcoef.shape, kcoef.dtype),
            pltpu.VMEM((1, gpoints), jnp.float32),
            pltpu.VMEM((columns, feats, levels), state.dtype),
            pltpu.VMEM((2 * gpoints, 2 * feats), jnp.bfloat16),
            pltpu.VMEM((wide, wide), jnp.bfloat16),
            pltpu.VMEM((gpoints, wide), jnp.float32),
            pltpu.VMEM((columns, gpoints // 2), jnp.float32),
            pltpu.VMEM((2 * gpoints, wide), jnp.float32),
            pltpu.VMEM((2 * gpoints, wide), jnp.float32),
            pltpu.VMEM((gpoints, wide), jnp.float32),
            pltpu.VMEM((gpoints, wide), jnp.float32),
            pltpu.VMEM((gpoints, wide), jnp.float32),
            pltpu.VMEM((gpoints, wide), jnp.float32),
            pltpu.VMEM((gpoints, wide), jnp.bfloat16),
            pltpu.VMEM((gpoints, wide), jnp.bfloat16),
            pltpu.VMEM((2, unroll, 8, wide), jnp.float32),
            pltpu.VMEM(cosine.shape, jnp.float32),
            pltpu.SemaphoreType.DMA((8,)),
        ],
        compiler_params=pltpu.CompilerParams(vmem_limit_bytes=60 * 1024 * 1024),
        cost_estimate=pl.CostEstimate(
            flops=columns * levels * gpoints * 600,
            bytes_accessed=columns * feats * levels * 2,
            transcendentals=columns * levels * gpoints * 6,
        ),
        name="radiation",
    )(cosine, sunlit, state, kcoef, scatter_coef, weights.reshape(1, -1))


def pick(rows, index):
    low = index % 128
    high = index // 128
    found = jnp.zeros(index.shape, jnp.float32)
    for row, line in enumerate(rows):
        line = jnp.broadcast_to(line, index.shape)
        found = jnp.where(high == row, jnp.take_along_axis(line, low, axis=1), found)
    return found


def ocean_kernel(
    flux_ref, icol_hbm, iweight_hbm, sea_hbm, sea_all,
    flux_all, icol_ref, iweight_ref, sea_ref, next_ref, local_sems, own_sem, send_flux, recv_flux, send_sea, recv_sea,
):
    sections, rows, _ = flux_all.shape
    me = lax.axis_index("cpl")
    others = [lax.rem(me + step, sections) for step in range(1, sections)]
    barrier = pltpu.get_barrier_semaphore()
    for other in others:
        pl.semaphore_signal(barrier, inc=1, device_id={"cpl": other}, device_id_type=pl.DeviceIdType.MESH)
    fetches = [
        pltpu.make_async_copy(source, target, local_sems.at[at])
        for at, (source, target) in enumerate(
            (
                (icol_hbm, icol_ref), (iweight_hbm, iweight_ref), (sea_hbm, sea_ref), (flux_ref, flux_all.at[me]),
            )
        )
    ]
    for fetch in fetches:
        fetch.start()
    pl.semaphore_wait(barrier, sections - 1)

    def spread(block, table, send, recv):
        copies = [
            pltpu.make_async_remote_copy(
                src_ref=block, dst_ref=table.at[me], send_sem=send.at[step], recv_sem=recv.at[step],
                device_id={"cpl": other}, device_id_type=pl.DeviceIdType.MESH,
            )
            for step, other in enumerate(others)
        ]
        for copy in copies:
            copy.start()
        return copies

    copies = spread(flux_ref, flux_all, send_flux, recv_flux)
    for fetch in fetches:
        fetch.wait()
    index = jnp.concatenate([icol_ref[:, 128 * j : 128 * (j + 1)] for j in range(rows)], axis=0)
    weight = jnp.concatenate([iweight_ref[:, 128 * j : 128 * (j + 1)] for j in range(rows)], axis=0)
    weight = weight.astype(jnp.float32)
    overlaps = icol_ref.shape[0]
    for copy in copies:
        copy.wait()
    lines = [flux_all[section, row : row + 1, :] for section in range(sections) for row in range(rows)]
    product = weight * pick(lines, index)
    for j in range(rows):
        part = slice(overlaps * j, overlaps * (j + 1))
        top = jnp.sum(product[part], axis=0, keepdims=True)
        bottom = jnp.sum(weight[part], axis=0, keepdims=True)
        next_ref[j : j + 1, :] = relax_keep * sea_ref[j : j + 1, :] + forcing * (top / bottom)
    copies = spread(next_ref, sea_all, send_sea, recv_sea)
    own = pltpu.make_async_copy(next_ref, sea_all.at[me], own_sem)
    own.start()
    for copy in copies:
        copy.wait()
    own.wait()


def ocean(flux, icol, iweight, sea):
    sections = lax.axis_size("cpl")
    table = (sections, *sea.shape)
    arrivals = pltpu.SemaphoreType.DMA((sections - 1,))
    return pl.pallas_call(
        ocean_kernel,
        out_shape=jax.ShapeDtypeStruct(table, jnp.float32),
        in_specs=[anywhere] * 4,
        out_specs=anywhere,
        scratch_shapes=[
            pltpu.VMEM(table, jnp.float32),
            pltpu.VMEM(icol.shape, icol.dtype),
            pltpu.VMEM(iweight.shape, iweight.dtype),
            pltpu.VMEM(sea.shape, jnp.float32),
            pltpu.VMEM(sea.shape, jnp.float32),
            pltpu.SemaphoreType.DMA((4,)),
            pltpu.SemaphoreType.DMA,
            arrivals, arrivals, arrivals, arrivals,
        ],
        compiler_params=pltpu.CompilerParams(
            collective_id=0, has_side_effects=True, vmem_limit_bytes=60 * 1024 * 1024
        ),
        name="ocean",
    )(flux, icol, iweight, sea)


def column_kernel(sea_all, near_ref, next_ref, column_ref):
    sections, rows, _ = sea_all.shape
    next_ref[...] = sea_all[lax.axis_index("cpl")]
    lines = [sea_all[section, row : row + 1, :] for section in range(sections) for row in range(rows)]
    column_ref[...] = pick(lines, near_ref[...])


def column(sea_all, near):
    shape = jax.ShapeDtypeStruct(sea_all.shape[1:], jnp.float32)
    return pl.pallas_call(
        column_kernel,
        out_shape=(shape, jax.ShapeDtypeStruct(near.shape, jnp.float32)),
        in_specs=[vmem] * 2,
        out_specs=(vmem, vmem),
        compiler_params=pltpu.CompilerParams(vmem_limit_bytes=60 * 1024 * 1024),
        name="column",
    )(sea_all, near)


def local(
    state, cosine_zenith, sunlit, kcoef, scatter_coef, gpoint_weight, sea_temp,
    intersection_col, intersection_weight, nearest_ocean,
):
    cosine = cosine_zenith.reshape(-1, 128)
    heating, surface = radiation(cosine, sunlit, state, kcoef, scatter_coef, gpoint_weight)
    sea_all = ocean(surface, intersection_col.T, intersection_weight.T, sea_temp.reshape(-1, 128))
    sea_next, column_sea = column(sea_all, nearest_ocean.reshape(-1, 128))
    return (heating, sea_next.reshape(-1), column_sea.reshape(-1))


def solution(mesh):
    both = ("atm", "cpl")
    return jax.shard_map(
        local,
        mesh=mesh,
        in_specs=(
            P(both, None, None), P(both), P(both), P(), P(), P(), P(both),
            P(both, None), P(both, None), P(both),
        ),
        out_specs=(P(both, None), P(both), P(both)),
        check_vma=False,
    )
```

```python
import functools

import jax
import jax.numpy as jnp
from jax import lax
from jax.experimental import pallas as pl
from jax.experimental.pallas import tpu as pltpu
from jax.sharding import PartitionSpec as P

depth_scale = 0.01
relax_keep = 0.75
forcing = 4.0
log2e = 1.4426950408889634
ln2 = 0.6931471805599453
one_up = 1.0 + 2.0**-23
small_row = 14.0
block_g = 32
unroll = 8
first_cols = 64


def radiation_kernel(
    cosine_hbm, sunlit_hbm, state_hbm, kcoef_hbm, scatter_hbm, weight_hbm,
    heat_hbm, surf_ref,
    heat_ref, cosine_vec, cosine_ref, sunlit_ref, kcoef_ref, scatter_ref, weight_ref, state_ref, kboth_ref, upper_ref, wide_ref, part_ref,
    proj0, proj1, a0, a1, x0, x1, ext0, ext1, rate_ref, cosine_f32, sems,
):
    columns, levels = heat_ref.shape
    gpoints = wide_ref.shape[0]
    pairs = columns // 2
    head = pltpu.make_async_copy(
        state_hbm.at[pl.ds(0, first_cols)], state_ref.at[pl.ds(0, first_cols)], sems.at[0]
    )
    tail = pltpu.make_async_copy(
        state_hbm.at[pl.ds(first_cols, columns - first_cols)],
        state_ref.at[pl.ds(first_cols, columns - first_cols)],
        sems.at[1],
    )
    small = [
        pltpu.make_async_copy(source, target, sems.at[2 + at])
        for at, (source, target) in enumerate(
            (
                (kcoef_hbm, kcoef_ref), (scatter_hbm, scatter_ref), (weight_hbm, weight_ref),
                (cosine_hbm, cosine_vec), (sunlit_hbm, sunlit_ref),
            )
        )
    ]
    for copy in small:
        copy.start()
    head.start()
    tail.start()
    row_index = lax.broadcasted_iota(jnp.int32, (2 * levels, 2 * levels), 0)
    col_index = lax.broadcasted_iota(jnp.int32, (2 * levels, 2 * levels), 1)
    same = (row_index >= levels) == (col_index >= levels)
    upper = jnp.where(same & (row_index <= col_index), 1.0, 0.0)
    upper_ref[...] = upper.astype(jnp.bfloat16)
    for copy in small:
        copy.wait()
    cosine_wide = cosine_vec[...].astype(jnp.float32)
    cosine_f32[...] = cosine_wide
    scalars = pltpu.make_async_copy(cosine_f32, cosine_ref, sems.at[7])
    scalars.start()

    for half, ref in enumerate((kcoef_ref, scatter_ref)):
        scaled = ref[...].astype(jnp.float32) * log2e
        high = scaled.astype(jnp.bfloat16).astype(jnp.float32)
        both = jnp.concatenate([high, scaled - high], axis=0)
        kboth_ref[pl.ds(half * gpoints, gpoints), :] = both.T.astype(jnp.bfloat16)
    wide_ref[...] = jnp.broadcast_to(weight_ref[...], (2 * levels, gpoints)).T
    reach = jnp.maximum(
        jnp.sum(jnp.abs(kcoef_ref[...].astype(jnp.float32)), axis=0, keepdims=True),
        jnp.sum(jnp.abs(scatter_ref[...].astype(jnp.float32)), axis=0, keepdims=True),
    )
    bounded = jnp.max(reach) <= small_row

    row_id = lax.broadcasted_iota(jnp.int32, (8, 2 * levels), 0)
    lane_id = lax.broadcasted_iota(jnp.int32, (8, 2 * levels), 1)
    left = lane_id < levels
    select = jnp.where((left & (row_id == 0)) | (~left & (row_id == 1)), 1.0, 0.0).astype(jnp.bfloat16)
    row8 = lax.broadcasted_iota(jnp.int32, (8, gpoints), 0)
    start = lax.broadcasted_iota(jnp.int32, (block_g, levels), 1) == 0
    lane1 = lax.broadcasted_iota(jnp.int32, (1, 2 * levels), 1)
    lane8 = lax.broadcasted_iota(jnp.int32, (8, 2 * levels), 1)

    def project(pair, proj):
        base = 2 * jnp.minimum(pair, pairs - 1)
        both = jnp.concatenate([state_ref[base], state_ref[base + 1]], axis=1)
        both = jnp.concatenate([both, both], axis=0)
        proj[...] = jnp.dot(kboth_ref[...], both, preferred_element_type=jnp.float32)

    def soften(clamped, proj, a_ref, x_ref, ext_ref):
        for low in range(0, gpoints, block_g):
            rows = slice(low, low + block_g)
            ta, ts = proj[rows], proj[gpoints + low : gpoints + low + block_g]
            ya = jnp.exp2(jnp.minimum(ta, 24.0) if clamped else ta)
            ys = jnp.exp2(jnp.minimum(ts, 24.0) if clamped else ts)
            soft_abs = jnp.minimum(lax.log2(ya + one_up), ya * log2e)
            soft_sca = lax.log2(ys + one_up)
            if clamped:
                soft_abs = jnp.maximum(ta, soft_abs)
                soft_sca = jnp.maximum(ts, soft_sca)
            soft = soft_abs + soft_sca
            a_ref[rows] = soft_abs
            x_ref[rows] = soft
            ext_ref[rows] = ((depth_scale * ln2) * soft).astype(jnp.bfloat16)

    def sun(base):
        line, lane = base // 128, lax.rem(base, 128)
        lit = [sunlit_ref[base + at] > 0 for at in range(2)]
        u = [jnp.where(lit[at], cosine_ref[line, lane + at], 1.0) for at in range(2)]
        return u, [jnp.where(lit[at], u[at], 0.0) for at in range(2)]

    def rates(first, count, bank):
        for at in range(count):
            u, _ = sun(2 * jnp.minimum(first + at, pairs - 1))
            rate_ref[bank, at] = -log2e / jnp.where(lane8 < levels, u[0], u[1])

    def absorb(pair, bank, at, a_ref, x_ref, ext_ref):
        base = 2 * pair
        _, out = sun(base)
        through = jnp.dot(ext_ref[...], upper_ref[...], preferred_element_type=jnp.float32)
        total = jnp.zeros((8, 2 * levels), jnp.float32)
        for low in range(0, gpoints, block_g):
            rows = slice(low, low + block_g)
            depth = through[rows].reshape(block_g // 8, 8, 2 * levels)
            leave = jnp.exp2((depth * rate_ref[bank, at][None]).reshape(block_g, 2 * levels))
            enter = jnp.concatenate(
                [
                    jnp.where(start, 1.0, pltpu.roll(leave[:, :levels], 1, 1)),
                    jnp.where(start, 1.0, pltpu.roll(leave[:, levels:], 1, 1)),
                ],
                axis=1,
            )
            top = a_ref[rows] * ((enter - leave) * wide_ref[rows])
            bottom = x_ref[rows]
            for half in (block_g // 2, block_g // 4):
                top, bottom = (
                    top[:half] * bottom[half:] + top[half:] * bottom[:half],
                    bottom[:half] * bottom[half:],
                )
            total = total + top * pl.reciprocal(bottom, approx=True)
        out_lane = jnp.where(lane1 < levels, out[0], out[1])
        row = jnp.sum(total, axis=0, keepdims=True) * (out_lane * (levels / gpoints))
        heat_ref[pl.ds(base, 1), :] = row[:, :levels]
        heat_ref[pl.ds(base + 1, 1), :] = row[:, levels:]

    def reach_ground(pair, ext_ref):
        base = 2 * pair
        u, out = sun(base)
        depth = lax.dot_general(
            select, ext_ref[...], (((1,), (1,)), ((), ())), preferred_element_type=jnp.float32
        )
        u_row = jnp.where(row8 == 0, u[0], u[1])
        out_row = jnp.where(row8 == 0, out[0], out[1])
        left_over = out_row * jnp.exp(-depth / u_row) * (weight_ref[...] / gpoints)
        half = left_over[:, : gpoints // 2] + left_over[:, gpoints // 2 :]
        part_ref[pl.ds(base, 1), :] = half[0:1]
        part_ref[pl.ds(base + 1, 1), :] = half[1:2]

    def sweep(clamped, together):
        projs, sets = (proj0, proj1), ((a0, x0, ext0), (a1, x1, ext1))
        rates(0, together, 0)
        project(0, projs[0])
        soften(clamped, projs[0], *sets[0])
        project(1, projs[1])

        def step(i, carry):
            @pl.when(i == 1)
            def _():
                tail.wait()

            bank = lax.rem(i, 2)
            for at in range(together):
                pair, now, later = together * i + at, at % 2, (at + 1) % 2
                absorb(pair, bank, at, *sets[now])
                reach_ground(pair, sets[now][2])
                soften(clamped, projs[later], *sets[later])
                project(pair + 2, projs[now])
                if at == 0:
                    rates(together * (i + 1), together, 1 - bank)
            return carry

        lax.fori_loop(0, pairs // together, step, jnp.int32(0))

    scalars.wait()
    head.wait()

    @pl.when(bounded)
    def _():
        sweep(False, unroll)

    @pl.when(jnp.logical_not(bounded))
    def _():
        sweep(True, 2)

    heat_out = pltpu.make_async_copy(heat_ref, heat_hbm, sems.at[8])
    heat_out.start()
    for block in range(columns // 128):
        piece = part_ref[block * 128 : (block + 1) * 128].T
        surf_ref[block : block + 1, :] = jnp.sum(piece, axis=0, keepdims=True)
    heat_out.wait()


vmem = pl.BlockSpec(memory_space=pltpu.VMEM)
smem = pl.BlockSpec(memory_space=pltpu.SMEM)
anywhere = pl.BlockSpec(memory_space=pl.ANY)


def radiation(cosine, sunlit, state, kcoef, scatter_coef, weights):
    columns, feats, levels = state.shape
    gpoints = kcoef.shape[1]
    wide = 2 * levels
    return pl.pallas_call(
        radiation_kernel,
        out_shape=(
            jax.ShapeDtypeStruct((columns, levels), jnp.float32),
            jax.ShapeDtypeStruct((columns // 128, 128), jnp.float32),
        ),
        in_specs=[anywhere] * 6,
        out_specs=(anywhere, vmem),
        scratch_shapes=[
            pltpu.VMEM((columns, levels), jnp.float32),
            pltpu.VMEM(cosine.shape, cosine.dtype),
            pltpu.SMEM(cosine.shape, jnp.float32),
            pltpu.SMEM(sunlit.shape, sunlit.dtype),
            pltpu.VMEM(kcoef.shape, kcoef.dtype),
            pltpu.VMEM(kcoef.shape, kcoef.dtype),
            pltpu.VMEM((1, gpoints), jnp.float32),
            pltpu.VMEM((columns, feats, levels), state.dtype),
            pltpu.VMEM((2 * gpoints, 2 * feats), jnp.bfloat16),
            pltpu.VMEM((wide, wide), jnp.bfloat16),
            pltpu.VMEM((gpoints, wide), jnp.float32),
            pltpu.VMEM((columns, gpoints // 2), jnp.float32),
            pltpu.VMEM((2 * gpoints, wide), jnp.float32),
            pltpu.VMEM((2 * gpoints, wide), jnp.float32),
            pltpu.VMEM((gpoints, wide), jnp.float32),
            pltpu.VMEM((gpoints, wide), jnp.float32),
            pltpu.VMEM((gpoints, wide), jnp.float32),
            pltpu.VMEM((gpoints, wide), jnp.float32),
            pltpu.VMEM((gpoints, wide), jnp.bfloat16),
            pltpu.VMEM((gpoints, wide), jnp.bfloat16),
            pltpu.VMEM((2, unroll, 8, wide), jnp.float32),
            pltpu.VMEM(cosine.shape, jnp.float32),
            pltpu.SemaphoreType.DMA((9,)),
        ],
        compiler_params=pltpu.CompilerParams(vmem_limit_bytes=60 * 1024 * 1024),
        cost_estimate=pl.CostEstimate(
            flops=columns * levels * gpoints * 600,
            bytes_accessed=columns * feats * levels * 2,
            transcendentals=columns * levels * gpoints * 6,
        ),
        name="radiation",
    )(cosine, sunlit, state, kcoef, scatter_coef, weights.reshape(1, -1))


def pick(rows, index):
    low = index % 128
    high = index // 128
    found = jnp.zeros(index.shape, jnp.float32)
    for row, line in enumerate(rows):
        line = jnp.broadcast_to(line, index.shape)
        found = jnp.where(high == row, jnp.take_along_axis(line, low, axis=1), found)
    return found


def ocean_kernel(
    flux_ref, icol_hbm, iweight_hbm, sea_hbm, sea_all,
    flux_all, icol_ref, iweight_ref, sea_ref, next_ref, local_sems, own_sem, send_flux, recv_flux, send_sea, recv_sea,
):
    sections, rows, _ = flux_all.shape
    me = lax.axis_index("cpl")
    others = [lax.rem(me + step, sections) for step in range(1, sections)]
    barrier = pltpu.get_barrier_semaphore()
    for other in others:
        pl.semaphore_signal(barrier, inc=1, device_id={"cpl": other}, device_id_type=pl.DeviceIdType.MESH)
    fetches = [
        pltpu.make_async_copy(source, target, local_sems.at[at])
        for at, (source, target) in enumerate(
            (
                (icol_hbm, icol_ref), (iweight_hbm, iweight_ref), (sea_hbm, sea_ref), (flux_ref, flux_all.at[me]),
            )
        )
    ]
    for fetch in fetches:
        fetch.start()
    pl.semaphore_wait(barrier, sections - 1)

    def spread(block, table, send, recv):
        copies = [
            pltpu.make_async_remote_copy(
                src_ref=block, dst_ref=table.at[me], send_sem=send.at[step], recv_sem=recv.at[step],
                device_id={"cpl": other}, device_id_type=pl.DeviceIdType.MESH,
            )
            for step, other in enumerate(others)
        ]
        for copy in copies:
            copy.start()
        return copies

    copies = spread(flux_ref, flux_all, send_flux, recv_flux)
    for fetch in fetches:
        fetch.wait()
    index = jnp.concatenate([icol_ref[:, 128 * j : 128 * (j + 1)] for j in range(rows)], axis=0)
    weight = jnp.concatenate([iweight_ref[:, 128 * j : 128 * (j + 1)] for j in range(rows)], axis=0)
    weight = weight.astype(jnp.float32)
    overlaps = icol_ref.shape[0]
    for copy in copies:
        copy.wait()
    lines = [flux_all[section, row : row + 1, :] for section in range(sections) for row in range(rows)]
    product = weight * pick(lines, index)
    for j in range(rows):
        part = slice(overlaps * j, overlaps * (j + 1))
        top = jnp.sum(product[part], axis=0, keepdims=True)
        bottom = jnp.sum(weight[part], axis=0, keepdims=True)
        next_ref[j : j + 1, :] = relax_keep * sea_ref[j : j + 1, :] + forcing * (top / bottom)
    copies = spread(next_ref, sea_all, send_sea, recv_sea)
    own = pltpu.make_async_copy(next_ref, sea_all.at[me], own_sem)
    own.start()
    for copy in copies:
        copy.wait()
    own.wait()


def ocean(flux, icol, iweight, sea):
    sections = lax.axis_size("cpl")
    table = (sections, *sea.shape)
    arrivals = pltpu.SemaphoreType.DMA((sections - 1,))
    return pl.pallas_call(
        ocean_kernel,
        out_shape=jax.ShapeDtypeStruct(table, jnp.float32),
        in_specs=[anywhere] * 4,
        out_specs=anywhere,
        scratch_shapes=[
            pltpu.VMEM(table, jnp.float32),
            pltpu.VMEM(icol.shape, icol.dtype),
            pltpu.VMEM(iweight.shape, iweight.dtype),
            pltpu.VMEM(sea.shape, jnp.float32),
            pltpu.VMEM(sea.shape, jnp.float32),
            pltpu.SemaphoreType.DMA((4,)),
            pltpu.SemaphoreType.DMA,
            arrivals, arrivals, arrivals, arrivals,
        ],
        compiler_params=pltpu.CompilerParams(
            collective_id=0, has_side_effects=True, vmem_limit_bytes=60 * 1024 * 1024
        ),
        name="ocean",
    )(flux, icol, iweight, sea)


def column_kernel(sea_all, near_ref, next_ref, column_ref):
    sections, rows, _ = sea_all.shape
    next_ref[...] = sea_all[lax.axis_index("cpl")]
    lines = [sea_all[section, row : row + 1, :] for section in range(sections) for row in range(rows)]
    column_ref[...] = pick(lines, near_ref[...])


def column(sea_all, near):
    shape = jax.ShapeDtypeStruct(sea_all.shape[1:], jnp.float32)
    return pl.pallas_call(
        column_kernel,
        out_shape=(shape, jax.ShapeDtypeStruct(near.shape, jnp.float32)),
        in_specs=[vmem] * 2,
        out_specs=(vmem, vmem),
        compiler_params=pltpu.CompilerParams(vmem_limit_bytes=60 * 1024 * 1024),
        name="column",
    )(sea_all, near)


def local(
    state, cosine_zenith, sunlit, kcoef, scatter_coef, gpoint_weight, sea_temp,
    intersection_col, intersection_weight, nearest_ocean,
):
    cosine = cosine_zenith.reshape(-1, 128)
    heating, surface = radiation(cosine, sunlit, state, kcoef, scatter_coef, gpoint_weight)
    sea_all = ocean(surface, intersection_col.T, intersection_weight.T, sea_temp.reshape(-1, 128))
    sea_next, column_sea = column(sea_all, nearest_ocean.reshape(-1, 128))
    return (heating, sea_next.reshape(-1), column_sea.reshape(-1))


def solution(mesh):
    both = ("atm", "cpl")
    return jax.shard_map(
        local,
        mesh=mesh,
        in_specs=(
            P(both, None, None), P(both), P(both), P(), P(), P(), P(both),
            P(both, None), P(both, None), P(both),
        ),
        out_specs=(P(both, None), P(both), P(both)),
        check_vma=False,
    )
```

```python
import functools

import jax
import jax.numpy as jnp
from jax import lax
from jax.experimental import pallas as pl
from jax.experimental.pallas import tpu as pltpu
from jax.sharding import PartitionSpec as P

depth_scale = 0.01
relax_keep = 0.75
forcing = 4.0
log2e = 1.4426950408889634
ln2 = 0.6931471805599453
one_up = 1.0 + 2.0**-23
small_row = 14.0
block_g = 32
unroll = 8
first_cols = 64


def radiation_kernel(
    cosine_hbm, sunlit_hbm, state_hbm, kcoef_hbm, scatter_hbm, weight_hbm,
    heat_ref, surf_ref,
    cosine_vec, cosine_ref, sunlit_ref, kcoef_ref, scatter_ref, weight_ref, state_ref, kboth_ref, upper_ref, wide_ref, part_ref,
    proj0, proj1, a0, a1, x0, x1, ext0, ext1, rate_ref, cosine_f32, sems,
):
    columns, levels = heat_ref.shape
    gpoints = wide_ref.shape[0]
    pairs = columns // 2
    head = pltpu.make_async_copy(
        state_hbm.at[pl.ds(0, first_cols)], state_ref.at[pl.ds(0, first_cols)], sems.at[0]
    )
    tail = pltpu.make_async_copy(
        state_hbm.at[pl.ds(first_cols, columns - first_cols)],
        state_ref.at[pl.ds(first_cols, columns - first_cols)],
        sems.at[1],
    )
    small = [
        pltpu.make_async_copy(source, target, sems.at[2 + at])
        for at, (source, target) in enumerate(
            (
                (kcoef_hbm, kcoef_ref), (scatter_hbm, scatter_ref), (weight_hbm, weight_ref),
                (cosine_hbm, cosine_vec), (sunlit_hbm, sunlit_ref),
            )
        )
    ]
    for copy in small:
        copy.start()
    head.start()
    tail.start()
    row_index = lax.broadcasted_iota(jnp.int32, (2 * levels, 2 * levels), 0)
    col_index = lax.broadcasted_iota(jnp.int32, (2 * levels, 2 * levels), 1)
    same = (row_index >= levels) == (col_index >= levels)
    upper = jnp.where(same & (row_index <= col_index), 1.0, 0.0)
    upper_ref[...] = upper.astype(jnp.bfloat16)
    for copy in small:
        copy.wait()
    cosine_wide = cosine_vec[...].astype(jnp.float32)
    cosine_f32[...] = cosine_wide
    scalars = pltpu.make_async_copy(cosine_f32, cosine_ref, sems.at[7])
    scalars.start()

    for half, ref in enumerate((kcoef_ref, scatter_ref)):
        scaled = ref[...].astype(jnp.float32) * log2e
        high = scaled.astype(jnp.bfloat16).astype(jnp.float32)
        both = jnp.concatenate([high, scaled - high], axis=0)
        kboth_ref[pl.ds(half * gpoints, gpoints), :] = both.T.astype(jnp.bfloat16)
    wide_ref[...] = jnp.broadcast_to(weight_ref[...], (2 * levels, gpoints)).T
    reach = jnp.maximum(
        jnp.sum(jnp.abs(kcoef_ref[...].astype(jnp.float32)), axis=0, keepdims=True),
        jnp.sum(jnp.abs(scatter_ref[...].astype(jnp.float32)), axis=0, keepdims=True),
    )
    bounded = jnp.max(reach) <= small_row

    row_id = lax.broadcasted_iota(jnp.int32, (8, 2 * levels), 0)
    lane_id = lax.broadcasted_iota(jnp.int32, (8, 2 * levels), 1)
    left = lane_id < levels
    select = jnp.where((left & (row_id == 0)) | (~left & (row_id == 1)), 1.0, 0.0).astype(jnp.bfloat16)
    row8 = lax.broadcasted_iota(jnp.int32, (8, gpoints), 0)
    start = lax.broadcasted_iota(jnp.int32, (block_g, levels), 1) == 0
    lane1 = lax.broadcasted_iota(jnp.int32, (1, 2 * levels), 1)
    lane8 = lax.broadcasted_iota(jnp.int32, (8, 2 * levels), 1)

    def project(pair, proj):
        base = 2 * jnp.minimum(pair, pairs - 1)
        both = jnp.concatenate([state_ref[base], state_ref[base + 1]], axis=1)
        both = jnp.concatenate([both, both], axis=0)
        proj[...] = jnp.dot(kboth_ref[...], both, preferred_element_type=jnp.float32)

    def soften(clamped, proj, a_ref, x_ref, ext_ref):
        for low in range(0, gpoints, block_g):
            rows = slice(low, low + block_g)
            ta, ts = proj[rows], proj[gpoints + low : gpoints + low + block_g]
            ya = jnp.exp2(jnp.minimum(ta, 24.0) if clamped else ta)
            ys = jnp.exp2(jnp.minimum(ts, 24.0) if clamped else ts)
            soft_abs = jnp.minimum(lax.log2(ya + one_up), ya * log2e)
            soft_sca = lax.log2(ys + one_up)
            if clamped:
                soft_abs = jnp.maximum(ta, soft_abs)
                soft_sca = jnp.maximum(ts, soft_sca)
            soft = soft_abs + soft_sca
            a_ref[rows] = soft_abs
            x_ref[rows] = soft
            ext_ref[rows] = ((depth_scale * ln2) * soft).astype(jnp.bfloat16)

    def sun(base):
        line, lane = base // 128, lax.rem(base, 128)
        lit = [sunlit_ref[base + at] > 0 for at in range(2)]
        u = [jnp.where(lit[at], cosine_ref[line, lane + at], 1.0) for at in range(2)]
        return u, [jnp.where(lit[at], u[at], 0.0) for at in range(2)]

    def rates(first, count, bank):
        for at in range(count):
            u, _ = sun(2 * jnp.minimum(first + at, pairs - 1))
            rate_ref[bank, at] = -log2e / jnp.where(lane8 < levels, u[0], u[1])

    def absorb(pair, bank, at, a_ref, x_ref, ext_ref):
        base = 2 * pair
        _, out = sun(base)
        through = jnp.dot(ext_ref[...], upper_ref[...], preferred_element_type=jnp.float32)
        total = jnp.zeros((8, 2 * levels), jnp.float32)
        for low in range(0, gpoints, block_g):
            rows = slice(low, low + block_g)
            depth = through[rows].reshape(block_g // 8, 8, 2 * levels)
            leave = jnp.exp2((depth * rate_ref[bank, at][None]).reshape(block_g, 2 * levels))
            enter = jnp.concatenate(
                [
                    jnp.where(start, 1.0, pltpu.roll(leave[:, :levels], 1, 1)),
                    jnp.where(start, 1.0, pltpu.roll(leave[:, levels:], 1, 1)),
                ],
                axis=1,
            )
            top = a_ref[rows] * ((enter - leave) * wide_ref[rows])
            bottom = x_ref[rows]
            for half in (block_g // 2, block_g // 4):
                top, bottom = (
                    top[:half] * bottom[half:] + top[half:] * bottom[:half],
                    bottom[:half] * bottom[half:],
                )
            total = total + top * pl.reciprocal(bottom, approx=True)
        out_lane = jnp.where(lane1 < levels, out[0], out[1])
        row = jnp.sum(total, axis=0, keepdims=True) * (out_lane * (levels / gpoints))
        heat_ref[pl.ds(base, 1), :] = row[:, :levels]
        heat_ref[pl.ds(base + 1, 1), :] = row[:, levels:]

    def reach_ground(pair, ext_ref):
        base = 2 * pair
        u, out = sun(base)
        depth = lax.dot_general(
            select, ext_ref[...], (((1,), (1,)), ((), ())), preferred_element_type=jnp.float32
        )
        u_row = jnp.where(row8 == 0, u[0], u[1])
        out_row = jnp.where(row8 == 0, out[0], out[1])
        left_over = out_row * jnp.exp(-depth / u_row) * (weight_ref[...] / gpoints)
        half = left_over[:, : gpoints // 2] + left_over[:, gpoints // 2 :]
        part_ref[pl.ds(base, 1), :] = half[0:1]
        part_ref[pl.ds(base + 1, 1), :] = half[1:2]

    def sweep(clamped, together):
        projs, sets = (proj0, proj1), ((a0, x0, ext0), (a1, x1, ext1))
        rates(0, together, 0)
        project(0, projs[0])
        soften(clamped, projs[0], *sets[0])
        project(1, projs[1])

        def step(i, carry):
            @pl.when(i == 1)
            def _():
                tail.wait()

            bank = lax.rem(i, 2)
            for at in range(together):
                pair, now, later = together * i + at, at % 2, (at + 1) % 2
                absorb(pair, bank, at, *sets[now])
                reach_ground(pair, sets[now][2])
                soften(clamped, projs[later], *sets[later])
                project(pair + 2, projs[now])
                if at == 0:
                    rates(together * (i + 1), together, 1 - bank)
            return carry

        lax.fori_loop(0, pairs // together, step, jnp.int32(0))

    scalars.wait()
    head.wait()

    @pl.when(bounded)
    def _():
        sweep(False, unroll)

    @pl.when(jnp.logical_not(bounded))
    def _():
        sweep(True, 2)

    for block in range(columns // 128):
        piece = part_ref[block * 128 : (block + 1) * 128].T
        surf_ref[block : block + 1, :] = jnp.sum(piece, axis=0, keepdims=True)


vmem = pl.BlockSpec(memory_space=pltpu.VMEM)
smem = pl.BlockSpec(memory_space=pltpu.SMEM)
anywhere = pl.BlockSpec(memory_space=pl.ANY)


def radiation(cosine, sunlit, state, kcoef, scatter_coef, weights):
    columns, feats, levels = state.shape
    gpoints = kcoef.shape[1]
    wide = 2 * levels
    return pl.pallas_call(
        radiation_kernel,
        out_shape=(
            jax.ShapeDtypeStruct((columns, levels), jnp.float32),
            jax.ShapeDtypeStruct((columns // 128, 128), jnp.float32),
        ),
        in_specs=[anywhere] * 6,
        out_specs=(vmem, vmem),
        scratch_shapes=[
            pltpu.VMEM(cosine.shape, cosine.dtype),
            pltpu.SMEM(cosine.shape, jnp.float32),
            pltpu.SMEM(sunlit.shape, sunlit.dtype),
            pltpu.VMEM(kcoef.shape, kcoef.dtype),
            pltpu.VMEM(kcoef.shape, kcoef.dtype),
            pltpu.VMEM((1, gpoints), jnp.float32),
            pltpu.VMEM((columns, feats, levels), state.dtype),
            pltpu.VMEM((2 * gpoints, 2 * feats), jnp.bfloat16),
            pltpu.VMEM((wide, wide), jnp.bfloat16),
            pltpu.VMEM((gpoints, wide), jnp.float32),
            pltpu.VMEM((columns, gpoints // 2), jnp.float32),
            pltpu.VMEM((2 * gpoints, wide), jnp.float32),
            pltpu.VMEM((2 * gpoints, wide), jnp.float32),
            pltpu.VMEM((gpoints, wide), jnp.float32),
            pltpu.VMEM((gpoints, wide), jnp.float32),
            pltpu.VMEM((gpoints, wide), jnp.float32),
            pltpu.VMEM((gpoints, wide), jnp.float32),
            pltpu.VMEM((gpoints, wide), jnp.bfloat16),
            pltpu.VMEM((gpoints, wide), jnp.bfloat16),
            pltpu.VMEM((2, unroll, 8, wide), jnp.float32),
            pltpu.VMEM(cosine.shape, jnp.float32),
            pltpu.SemaphoreType.DMA((8,)),
        ],
        compiler_params=pltpu.CompilerParams(vmem_limit_bytes=60 * 1024 * 1024),
        cost_estimate=pl.CostEstimate(
            flops=columns * levels * gpoints * 600,
            bytes_accessed=columns * feats * levels * 2,
            transcendentals=columns * levels * gpoints * 6,
        ),
        name="radiation",
    )(cosine, sunlit, state, kcoef, scatter_coef, weights.reshape(1, -1))


def places(index):
    return lax.shift_right_logical(index, 7), index & 127


def pick(rows, high, low):
    found = jnp.zeros(low.shape, jnp.float32)
    for row, line in enumerate(rows):
        line = jnp.broadcast_to(line, low.shape)
        found = jnp.where(high == row, jnp.take_along_axis(line, low, axis=1), found)
    return found


def ocean_kernel(
    flux_ref, icol_hbm, iweight_hbm, sea_hbm, sea_all,
    flux_all, icol_ref, iweight_ref, sea_ref, next_ref, local_sems, own_sem, send_flux, recv_flux, send_sea, recv_sea,
):
    sections, rows, _ = flux_all.shape
    me = lax.axis_index("cpl")
    others = [lax.rem(me + step, sections) for step in range(1, sections)]
    barrier = pltpu.get_barrier_semaphore()
    for other in others:
        pl.semaphore_signal(barrier, inc=1, device_id={"cpl": other}, device_id_type=pl.DeviceIdType.MESH)
    fetches = [
        pltpu.make_async_copy(source, target, local_sems.at[at])
        for at, (source, target) in enumerate(
            (
                (icol_hbm, icol_ref), (iweight_hbm, iweight_ref), (sea_hbm, sea_ref), (flux_ref, flux_all.at[me]),
            )
        )
    ]
    for fetch in fetches:
        fetch.start()
    pl.semaphore_wait(barrier, sections - 1)

    def spread(block, table, send, recv):
        copies = [
            pltpu.make_async_remote_copy(
                src_ref=block, dst_ref=table.at[me], send_sem=send.at[step], recv_sem=recv.at[step],
                device_id={"cpl": other}, device_id_type=pl.DeviceIdType.MESH,
            )
            for step, other in enumerate(others)
        ]
        for copy in copies:
            copy.start()
        return copies

    copies = spread(flux_ref, flux_all, send_flux, recv_flux)
    for fetch in fetches:
        fetch.wait()
    index = jnp.concatenate([icol_ref[:, 128 * j : 128 * (j + 1)] for j in range(rows)], axis=0)
    weight = jnp.concatenate([iweight_ref[:, 128 * j : 128 * (j + 1)] for j in range(rows)], axis=0)
    weight = weight.astype(jnp.float32)
    overlaps = icol_ref.shape[0]
    high, low = places(index)
    parts = [slice(overlaps * j, overlaps * (j + 1)) for j in range(rows)]
    bottoms = [jnp.sum(weight[part], axis=0, keepdims=True) for part in parts]
    kept = relax_keep * sea_ref[...]
    for copy in copies:
        copy.wait()
    lines = [flux_all[section, row : row + 1, :] for section in range(sections) for row in range(rows)]
    product = weight * pick(lines, high, low)
    for j, part in enumerate(parts):
        top = jnp.sum(product[part], axis=0, keepdims=True)
        next_ref[j : j + 1, :] = kept[j : j + 1] + forcing * (top / bottoms[j])
    copies = spread(next_ref, sea_all, send_sea, recv_sea)
    own = pltpu.make_async_copy(next_ref, sea_all.at[me], own_sem)
    own.start()
    for copy in copies:
        copy.wait()
    own.wait()


def ocean(flux, icol, iweight, sea):
    sections = lax.axis_size("cpl")
    table = (sections, *sea.shape)
    arrivals = pltpu.SemaphoreType.DMA((sections - 1,))
    return pl.pallas_call(
        ocean_kernel,
        out_shape=jax.ShapeDtypeStruct(table, jnp.float32),
        in_specs=[anywhere] * 4,
        out_specs=anywhere,
        scratch_shapes=[
            pltpu.VMEM(table, jnp.float32),
            pltpu.VMEM(icol.shape, icol.dtype),
            pltpu.VMEM(iweight.shape, iweight.dtype),
            pltpu.VMEM(sea.shape, jnp.float32),
            pltpu.VMEM(sea.shape, jnp.float32),
            pltpu.SemaphoreType.DMA((4,)),
            pltpu.SemaphoreType.DMA,
            arrivals, arrivals, arrivals, arrivals,
        ],
        compiler_params=pltpu.CompilerParams(
            collective_id=0, has_side_effects=True, vmem_limit_bytes=60 * 1024 * 1024
        ),
        name="ocean",
    )(flux, icol, iweight, sea)


def column_kernel(sea_all, near_ref, next_ref, column_ref):
    sections, rows, _ = sea_all.shape
    next_ref[...] = sea_all[lax.axis_index("cpl")]
    lines = [sea_all[section, row : row + 1, :] for section in range(sections) for row in range(rows)]
    column_ref[...] = pick(lines, *places(near_ref[...]))


def column(sea_all, near):
    shape = jax.ShapeDtypeStruct(sea_all.shape[1:], jnp.float32)
    return pl.pallas_call(
        column_kernel,
        out_shape=(shape, jax.ShapeDtypeStruct(near.shape, jnp.float32)),
        in_specs=[vmem] * 2,
        out_specs=(vmem, vmem),
        compiler_params=pltpu.CompilerParams(vmem_limit_bytes=60 * 1024 * 1024),
        name="column",
    )(sea_all, near)


def local(
    state, cosine_zenith, sunlit, kcoef, scatter_coef, gpoint_weight, sea_temp,
    intersection_col, intersection_weight, nearest_ocean,
):
    cosine = cosine_zenith.reshape(-1, 128)
    heating, surface = radiation(cosine, sunlit, state, kcoef, scatter_coef, gpoint_weight)
    sea_all = ocean(surface, intersection_col.T, intersection_weight.T, sea_temp.reshape(-1, 128))
    sea_next, column_sea = column(sea_all, nearest_ocean.reshape(-1, 128))
    return (heating, sea_next.reshape(-1), column_sea.reshape(-1))


def solution(mesh):
    both = ("atm", "cpl")
    return jax.shard_map(
        local,
        mesh=mesh,
        in_specs=(
            P(both, None, None), P(both), P(both), P(), P(), P(), P(both),
            P(both, None), P(both, None), P(both),
        ),
        out_specs=(P(both, None), P(both), P(both)),
        check_vma=False,
    )
```
